32 devices in a mesh: groups: 2 (over y), ctx: 4 (over z), head: 2 (over x), sub: 2 (over core).
Axes of the slice: x: 2, y: 2, z: 4, core: 2. Of those that a mesh axis runs over, the one named last changes fastest.
Arguments:
- queries: bfloat16 [3072, 8192], P(('groups', 'ctx'), ('head', 'sub')), parts along dimension 0, may hold values from -60 to 60
- key_rows: bfloat16 [3072, 1024], P(('groups', 'ctx'), 'head'), parts along dimension 0, may hold values from -6 to 6
- value_rows: bfloat16 [3072, 1024], P(('groups', 'ctx'), 'head'), parts along dimension 0, may hold values from -6 to 6
- out_weight: bfloat16 [8192, 5120], P(('head', 'sub'), 'ctx'), may hold values from -0.375 to 0.375
Outputs:
- mixed: bfloat16 [3072, 5120], P(('groups', 'ctx'), ('head', 'sub')), parts along dimension 0
The draws below stay inside these ranges and needn't reach their ends.
There are 2 independent parts, one for each index of `groups`. The reference program is written for one: setup_inputs(seed, part) draws one part's arguments, and reference() takes and returns one part's arrays. A program takes and returns all parts, laid end to end along the dimension named above; an argument that names none is the same for every part. Nothing has to cross between parts.
All inputs are finite; a program needn't handle non-finite values.
Results may differ from the reference program's by a relative error of at most 0.02.
Values may be sent and summed in bfloat16 or wider, within the bound.
A program may use at most 128 MiB of HBM per device.

```python
import jax
import jax.numpy as jnp
from jax import lax

D = 5120
QH = 64
KVH = 8
HD = 128
TOKENS = 1536
QPD = 16
N_HEAD = 2
N_SUB = 2


def paired_draw(key):
    key_base = jax.random.fold_in(key, 701)
    query_base = jax.random.fold_in(key, 702)
    keys_out = jnp.clip(jax.random.normal(key_base, (TOKENS, KVH * HD), jnp.float32), -6.0, 6.0)
    queries_out = 1.5 * jnp.clip(jax.random.normal(query_base, (TOKENS, QH * HD), jnp.float32), -6.0, 6.0)
    return (queries_out, keys_out)


def draw_queries(key, part):
    return paired_draw(key)[0].astype(jnp.bfloat16)


def draw_key_rows(key, part):
    return paired_draw(key)[1].astype(jnp.bfloat16)


def steps_of(rng, extent, split, least, high):
    level, own = 1.0, jax.random.fold_in(rng, 6)
    for dim, blocks in split:
        steps = jnp.exp(jax.random.uniform(jax.random.fold_in(own, dim), (blocks,), jnp.float32, least / len(split), high / len(split)))
        level = level * jnp.repeat(steps, extent[dim] // blocks).reshape([-1 if axis == dim else 1 for axis in range(len(extent))])
    return level


def noise(key, shape, spread, most, pieces=(), kind=jnp.bfloat16):
    level = steps_of(key, shape, pieces, -0.22, 0.18) if pieces else 1.0
    values = jax.random.normal(key, shape, jnp.float32) * spread * level
    return jnp.minimum(jnp.maximum(values, -most), most).astype(kind)


def setup_inputs(seed: int = 0, part: int = 0) -> dict:
    splits = jax.random.split(jax.random.key(seed), 5)
    part_splits = jax.random.split(jax.random.fold_in(splits[4], part), 5)
    return {
        "queries": draw_queries(jax.random.fold_in(jax.random.fold_in(splits[4], part), 71), part),
        "key_rows": draw_key_rows(jax.random.fold_in(jax.random.fold_in(splits[4], part), 71), part),
        "value_rows": noise(part_splits[2], (TOKENS, KVH * HD), 1.0, 6.0, ((0, 4), (1, 2))),
        "out_weight": noise(splits[3], (QH * HD, D), (QH * HD // 32) ** -0.5, 0.375, ((0, 4), (1, 4))),
    }


def reference(queries, key_rows, value_rows, out_weight):
    group_ratio = QH // KVH
    query_heads = queries.reshape(TOKENS, QH, HD)
    key_heads = key_rows.reshape(TOKENS, KVH, HD)
    value_heads = value_rows.reshape(TOKENS, KVH, HD)
    factor = 1.0 / (HD ** 0.5)

    def one_head(head_id):
        kv_id = head_id // group_ratio
        q_head = lax.dynamic_index_in_dim(query_heads, head_id, 1, keepdims=False)
        k_head = lax.dynamic_index_in_dim(key_heads, kv_id, 1, keepdims=False)
        v_head = lax.dynamic_index_in_dim(value_heads, kv_id, 1, keepdims=False)
        scores = jnp.dot(q_head, k_head.T, preferred_element_type=jnp.float32) * factor
        row_max = jnp.max(scores, axis=1, keepdims=True)
        expo = jnp.exp(scores - row_max)
        weights = expo.astype(jnp.bfloat16)
        summed = jnp.dot(weights, v_head, preferred_element_type=jnp.float32)
        return (summed / jnp.sum(expo, axis=1, keepdims=True)).astype(jnp.bfloat16)

    per_head = lax.map(one_head, jnp.arange(QH, dtype=jnp.int32))
    attended = jnp.transpose(per_head, (1, 0, 2)).reshape(TOKENS, QH * HD)
    width = QPD * HD

    def add_group(total, group_id):
        offset = (group_id * width).astype(jnp.int32)
        cols = lax.dynamic_slice_in_dim(attended, offset, width, 1)
        rows = lax.dynamic_slice_in_dim(out_weight, offset, width, 0)
        partial_value = jnp.dot(cols, rows, preferred_element_type=jnp.float32).astype(jnp.bfloat16)
        return total + partial_value.astype(jnp.float32), None

    total, _ = lax.scan(add_group, jnp.zeros((TOKENS, D), jnp.float32), jnp.arange(N_HEAD * N_SUB, dtype=jnp.int32))
    return total.astype(jnp.bfloat16)
```

```python
import functools
import math

import jax
import jax.numpy as jnp
from jax import lax
from jax.experimental import pallas as pl
from jax.experimental.pallas import tpu as pltpu
from jax.sharding import PartitionSpec as P

QH = 64
KVH = 8
HD = 128
CHUNKS = 8
TILE = 256
ROWS = 128
MESH = pl.DeviceIdType.MESH
BLOCK = 128
EARLY = 2
ORDER = ("w", "w", "w", "w", "w", 0, 1, "w", "w", 2, "w", "w", "w")


def kernel(
    n, n_head, per_pair, pairs, chunks, parts, k_hbm, v_hbm, q_hbm, w_hbm, o_ref,
    kv_all, v_ext, q_ref, att, w, own, out, rx1, summed, rx2, final,
    load_sems, kv_send, kv_recv, a_send, a_recv, s1, r1, s2, r2, s3, r3,
):
    me, head, sub = (lax.axis_index(a) for a in ("ctx", "head", "sub"))
    other = 1 - sub
    hs = head * 2 + sub
    tokens, width = q_ref.shape
    heads = width // HD
    columns = w.shape[1]
    piece = width // chunks
    to_right, to_left = me < n - 1, me > 0
    right, left = lax.min(me + 1, n - 1), lax.max(me - 1, 0)
    away = hs != me
    share = tokens // n_head

    def rows_of(b):
        return pl.ds(pl.multiple_of(b * tokens, tokens), tokens)

    first = pl.multiple_of((sub * heads // (QH // KVH)) * HD, HD)
    loads = [
        pltpu.make_async_copy(
            side.at[:, pl.ds(first, pairs * HD)],
            kv_all.at[rows_of(me), pl.ds(i * pairs * HD, pairs * HD)],
            load_sems.at[i],
        )
        for i, side in enumerate((k_hbm, v_hbm))
    ]
    loads.append(pltpu.make_async_copy(q_hbm, q_ref, load_sems.at[2]))
    loads.append(pltpu.make_async_copy(w_hbm, w, load_sems.at[3]))
    for load in loads:
        load.start()

    barrier = pltpu.get_barrier_semaphore()

    def greet(where):
        pl.semaphore_signal(barrier, inc=1, device_id=where, device_id_type=MESH)

    pl.when(to_right)(lambda: greet({"ctx": right}))
    pl.when(to_left)(lambda: greet({"ctx": left}))
    for h in range(n_head):
        source = {"ctx": hs, "head": h, "sub": me % 2}
        pl.when(jnp.logical_or(away, head != h))(functools.partial(greet, source))
    greet({"sub": other})
    for step in range(1, n_head):
        greet({"head": lax.rem(head + step, n_head)})
    count = 2 * n_head - 1 + to_right.astype(jnp.int32) + to_left.astype(jnp.int32)
    pl.semaphore_wait(barrier, count + away.astype(jnp.int32))

    def remote(src, dst, send, recv, where):
        return pltpu.make_async_remote_copy(
            src_ref=src, dst_ref=dst, send_sem=send, recv_sem=recv, device_id=where, device_id_type=MESH
        )

    def kv_copy(b, way, d):
        where = {"ctx": right if way == 0 else left}
        part = kv_all.at[rows_of(b)]
        return remote(part, part, kv_send.at[way, d], kv_recv.at[b], where)

    loads[0].wait()
    loads[1].wait()
    pl.when(to_right)(lambda: kv_copy(me, 0, 0).start())
    pl.when(to_left)(lambda: kv_copy(me, 1, 0).start())

    @pl.loop(1, n)
    def _(d):
        @pl.when(me - d >= 0)
        def _():
            copy = kv_copy(me - d, 0, d)
            copy.wait_recv()
            pl.when(to_right)(lambda: copy.start())

        @pl.when(me + d < n)
        def _():
            copy = kv_copy(me + d, 1, d)
            copy.wait_recv()
            pl.when(to_left)(lambda: copy.start())

    loads[2].wait()

    def a_copy(b, j, way, d):
        where = {"ctx": right if way == 0 else left}
        part = att.at[b, :, pl.ds(j * piece, piece)]
        return remote(part, part, a_send.at[way, d, j], a_recv.at[b, j], where)

    factor = math.log2(math.e) / HD**0.5
    for j in range(chunks):
        if j % (chunks // pairs) == 0:
            p = j // (chunks // pairs)
            v_ext[p, :, :HD] = kv_all[:, (pairs + p) * HD : (pairs + p + 1) * HD]
            v_ext[p, :, HD:] = jnp.ones((v_ext.shape[1], HD), v_ext.dtype)

        @pl.loop(j * heads // chunks, (j + 1) * heads // chunks)
        def _(h):
            pair = h // per_pair
            cols = pl.ds(pl.multiple_of(h * HD, HD), HD)
            keys = kv_all[:, pl.ds(pl.multiple_of(pair * HD, HD), HD)]
            for start in range(0, tokens, ROWS):
                rows = pl.ds(start, ROWS)
                scores = lax.dot_general(
                    q_ref[rows, cols], keys, (((1,), (1,)), ((), ())), preferred_element_type=jnp.float32
                )
                row_max = jnp.max(scores, axis=1, keepdims=True)
                weights = jnp.exp2((scores - row_max) * factor).astype(jnp.bfloat16)
                both = jnp.dot(weights, v_ext[pair], preferred_element_type=jnp.float32)
                att[me, rows, cols] = (both[:, :HD] / both[:, HD:]).astype(att.dtype)

        pl.when(to_right)(lambda: a_copy(me, j, 0, 0).start())
        pl.when(to_left)(lambda: a_copy(me, j, 1, 0).start())

    loads[3].wait()
    tile = columns // parts

    def cols_of(c):
        return pl.ds(0, columns) if parts == 1 else pl.ds(pl.multiple_of(c * tile, tile), tile)

    def core_copy(g, c):
        cols = cols_of(c)
        return remote(out.at[g, :, cols], rx1.at[g, :, cols], s1.at[g, c], r1.at[g, c], {"sub": other})

    def share_of(h):
        return pl.ds(pl.multiple_of(h * share, share), share)

    def head_copy(g, step, c):
        cols, target = cols_of(c), lax.rem(head + step, n_head)
        return remote(
            summed.at[g, share_of(target), cols], rx2.at[g, head, :, cols],
            s2.at[g, step - 1, c], r2.at[g, head, c], {"head": target},
        )

    def head_arrival(g, source, c):
        cols = cols_of(c)
        return remote(
            summed.at[g, share_of(source), cols], rx2.at[g, source, :, cols],
            s2.at[g, 0, c], r2.at[g, source, c], {"head": source},
        )

    def last_copy(g, h, c):
        cols = cols_of(c)
        where = {"ctx": 2 * g + sub, "head": me // 2, "sub": me % 2}
        return remote(final.at[g, :, cols], o_ref.at[share_of(h), cols], s3.at[g, c], r3.at[h, c], where)

    def product(t, c):
        cols = cols_of(c)
        return jnp.dot(att[t], w[:, cols], preferred_element_type=jnp.float32).astype(out.dtype)

    def multiply(t):
        g = t // 2

        @pl.when(t % 2 == sub)
        def _():
            @pl.loop(0, parts)
            def _(c):
                own[g, :, cols_of(c)] = product(t, c)

        @pl.when(t % 2 != sub)
        def _():
            @pl.loop(0, parts)
            def _(c):
                out[g, :, cols_of(c)] = product(t, c)
                core_copy(g, c).start()

    def combine(t):
        g = t // 2

        @pl.when(t % 2 == sub)
        def _():
            @pl.loop(0, parts)
            def _(c):
                cols = cols_of(c)
                core_copy(g, c).wait_recv()
                total = own[g, :, cols].astype(jnp.float32) + rx1[g, :, cols].astype(jnp.float32)
                summed[g, :, cols] = total.astype(summed.dtype)
                for step in range(1, n_head):
                    head_copy(g, step, c).start()

    def finish(t):
        g = t // 2

        @pl.when(t % 2 == sub)
        def _():
            @pl.loop(0, parts)
            def _(c):
                cols = cols_of(c)
                total = summed[g, share_of(head), cols].astype(jnp.float32)
                for step in range(1, n_head):
                    source = lax.rem(head + step, n_head)
                    head_arrival(g, source, c).wait_recv()
                    total += rx2[g, source, :, cols].astype(jnp.float32)
                final[g, :, cols] = total.astype(final.dtype)
                pl.when(jnp.logical_or(away, t != me))(lambda: last_copy(g, head, c).start())

    def finish_at(d):
        pl.when(jnp.logical_and(d >= 0, me - d >= 0))(lambda: finish(me - d))
        pl.when(jnp.logical_and(d > 0, me + d < n))(lambda: finish(me + d))

    def after(d, j, last=False):
        behind, ahead = me - d + 1, me + d - 1
        if j == 0:
            pl.when(behind >= 0)(lambda: multiply(behind))
        if j == chunks // 4:
            pl.when(jnp.logical_and(ahead < n, d > 1))(lambda: multiply(ahead))
        if j == chunks // 2:
            pl.when(behind >= 0)(lambda: combine(behind))
        if j == chunks // 2 + 1:
            pl.when(jnp.logical_and(ahead < n, d > 1))(lambda: combine(ahead))
        if j == chunks - 1 and not last:
            finish_at(d - 2)

    @pl.loop(1, n)
    def _(d):
        for j in range(chunks):

            @pl.when(me - d >= 0)
            def _():
                copy = a_copy(me - d, j, 0, d)
                copy.wait_recv()
                pl.when(to_right)(lambda: copy.start())

            @pl.when(me + d < n)
            def _():
                copy = a_copy(me + d, j, 1, d)
                copy.wait_recv()
                pl.when(to_left)(lambda: copy.start())

            after(d, j)

    finish_at(n - 2)
    for j in range(chunks):
        after(n, j, last=True)
    finish_at(n - 1)

    @pl.when(jnp.logical_not(away))
    def _():
        keep = pltpu.make_async_copy(final.at[me // 2], o_ref.at[share_of(head)], load_sems.at[0])
        keep.start()
        keep.wait()

    for h in range(n_head):

        @pl.when(jnp.logical_or(away, head != h))
        def _():
            @pl.loop(0, parts)
            def _(c):
                last_copy(0, h, c).wait_recv()

    @pl.loop(0, n)
    def _(d):
        for way, fits, go in ((0, me - d >= 0, to_right), (1, me + d < n, to_left)):
            b = me - d if way == 0 else me + d

            @pl.when(jnp.logical_and(fits, go))
            def _():
                kv_copy(b, way, d).wait_send()
                for j in range(chunks):
                    a_copy(b, j, way, d).wait_send()

    @pl.loop(0, n // 2)
    def _(g):
        @pl.loop(0, parts)
        def _(c):
            core_copy(g, c).wait_send()
            for step in range(1, n_head):
                head_copy(g, step, c).wait_send()
            pl.when(jnp.logical_or(away, 2 * g + sub != me))(lambda: last_copy(g, head, c).wait_send())


def on_device(queries, key_rows, value_rows, out_weight):
    tokens, width = queries.shape
    heads_here = width // HD
    group_ratio = QH // KVH
    pairs = max(heads_here // group_ratio, 1)
    per_pair = heads_here // pairs
    n = lax.axis_size("ctx")
    n_head = lax.axis_size("head")
    columns = out_weight.shape[1]
    block = (tokens, columns)
    groups = (n // 2,) + block
    chunks = min(CHUNKS, heads_here)
    parts = columns // TILE if columns % TILE == 0 else 1
    anywhere = pl.BlockSpec(memory_space=pl.ANY)
    dma = pltpu.SemaphoreType.DMA
    bf16 = jnp.bfloat16
    return pl.pallas_call(
        functools.partial(kernel, n, n_head, per_pair, pairs, chunks, parts),
        out_shape=jax.ShapeDtypeStruct(block, bf16),
        in_specs=[anywhere] * 4,
        out_specs=anywhere,
        scratch_shapes=[
            pltpu.VMEM((n * tokens, 2 * pairs * HD), bf16),
            pltpu.VMEM((pairs, n * tokens, 2 * HD), bf16),
            pltpu.VMEM((tokens, width), bf16),
            pltpu.VMEM((n, tokens, width), bf16),
            pltpu.VMEM(out_weight.shape, bf16),
            pltpu.VMEM(groups, bf16),
            pltpu.VMEM(groups, bf16),
            pltpu.VMEM(groups, bf16),
            pltpu.VMEM(groups, bf16),
            pltpu.VMEM((n // 2, n_head, tokens // n_head, columns), bf16),
            pltpu.VMEM((n // 2, tokens // n_head, columns), bf16),
            dma((4,)),
            dma((2, n)),
            dma((n,)),
            dma((2, n, chunks)),
            dma((n, chunks)),
            dma((n // 2, parts)),
            dma((n // 2, parts)),
            dma((n // 2, n_head - 1, parts)),
            dma((n // 2, n_head, parts)),
            dma((n // 2, parts)),
            dma((n_head, parts)),
        ],
        compiler_params=pltpu.CompilerParams(
            collective_id=0, has_side_effects=True, vmem_limit_bytes=60 * 2**20
        ),
    )(key_rows, value_rows, queries, out_weight)


def hub_kernel(
    n, n_head, per_pair, pairs, chunks, tile, k_hbm, v_hbm, q_hbm, w_hbm, o_ref,
    kv_all, v_ext, q_ref, att, w, w_far, part, rx1, rx2,
    load_sems, kv_send, kv_recv, a_send, a_recv, e_send, e_recv, f_send, f_recv,
    w_send, w_recv, y_send, y_recv, s1, r1, s2, r2, s3, r3,
):
    me, head, sub, group = (lax.axis_index(a) for a in ("ctx", "head", "sub", "groups"))
    tokens, width = q_ref.shape
    heads = width // HD
    columns = w.shape[1]
    blocks = tokens // BLOCK
    tiles = columns // tile
    pieces = 2 * tiles
    per_piece = width // 4
    low = n // 2 - 1
    is_hub = jnp.logical_and(me >= low, me <= low + 1)
    is_end = jnp.logical_not(is_hub)
    to_right, to_left = me < n - 1, me > 0
    right, left = lax.min(me + 1, n - 1), lax.max(me - 1, 0)
    other = n - 1 - me
    end = jnp.where(me <= low, 0, n - 1)
    far_end = n - 1 - end
    my_hub = jnp.where(me <= low, low, low + 1)
    side = me - low
    away_head, away_sub, away_group = 1 - head, 1 - sub, 1 - group

    def rows_of(b):
        return pl.ds(pl.multiple_of(b * tokens, tokens), tokens)

    first = pl.multiple_of((sub * heads // (QH // KVH)) * HD, HD)
    loads = []
    for p in range(pairs):
        for i, ref in enumerate((k_hbm, v_hbm)):
            loads.append(pltpu.make_async_copy(
                ref.at[:, pl.ds(pl.multiple_of(first + p * HD, HD), HD)],
                kv_all.at[rows_of(me), pl.ds((2 * p + i) * HD, HD)],
                load_sems.at[2 * p + i],
            ))
    load_w = pltpu.make_async_copy(w_hbm, w, load_sems.at[2 * pairs])
    load_q = pltpu.make_async_copy(q_hbm, q_ref, load_sems.at[2 * pairs + 1])
    for load in loads + [load_w, load_q]:
        load.start()

    barrier = pltpu.get_barrier_semaphore()

    def greet(where):
        pl.semaphore_signal(barrier, inc=1, device_id=where, device_id_type=MESH)

    pl.when(to_right)(lambda: greet({"ctx": right}))
    pl.when(to_left)(lambda: greet({"ctx": left}))
    greet({"sub": away_sub})
    greet({"head": away_head})
    greet({"groups": away_group})
    origin = low + head
    mine = jnp.logical_and(me == origin, sub == me % 2)
    for h in range(n_head):
        source = {"ctx": origin, "head": h, "sub": me % 2}
        pl.when(jnp.logical_not(jnp.logical_and(mine, head == h)))(functools.partial(greet, source))
    keeps = jnp.logical_and(is_hub, jnp.logical_and(head == side, sub == me % 2))
    count = 3 + to_right.astype(jnp.int32) + to_left.astype(jnp.int32)
    count += jnp.where(is_hub, 4, 0) - keeps.astype(jnp.int32)
    pl.semaphore_wait(barrier, count)

    def remote(src, dst, send, recv, where):
        return pltpu.make_async_remote_copy(
            src_ref=src, dst_ref=dst, send_sem=send, recv_sem=recv, device_id=where, device_id_type=MESH
        )

    def kv_copy(b, way, d, p):
        where = {"ctx": right if way == 0 else left}
        block = kv_all.at[rows_of(b), pl.ds(2 * p * HD, 2 * HD)]
        return remote(block, block, kv_send.at[way, d, p], kv_recv.at[b, p], where)

    for p in range(pairs):
        loads[2 * p].wait()
        loads[2 * p + 1].wait()
        pl.when(to_right)(lambda: kv_copy(me, 0, 0, p).start())
        pl.when(to_left)(lambda: kv_copy(me, 1, 0, p).start())

    def pass_on(d, p):
        @pl.when(me - d >= 0)
        def _():
            copy = kv_copy(me - d, 0, d, p)
            copy.wait_recv()
            pl.when(to_right)(lambda: copy.start())

        @pl.when(me + d < n)
        def _():
            copy = kv_copy(me + d, 1, d, p)
            copy.wait_recv()
            pl.when(to_left)(lambda: copy.start())

    def w_piece(g, i):
        rows = pl.ds(pl.multiple_of(g * (width // 2) + (i % 2) * per_piece, per_piece), per_piece)
        return rows, pl.ds((i // 2) * tile, tile)

    def w_copy(i):
        at = w_piece(group, i)
        return remote(w.at[at], w_far.at[at], w_send.at[i], w_recv.at[i], {"ctx": my_hub})

    def y_copy(g, i):
        at = w_piece(g, i)
        return remote(w_far.at[at], w_far.at[at], y_send.at[i], y_recv.at[i], {"groups": away_group})

    def relay_w(*which):
        for i in which:
            w_copy(i).wait_recv()
            y_copy(group, i).start()

    def await_w(*which):
        for i in which:
            y_copy(away_group, i).wait_recv()

    load_w.wait()
    ahead = ORDER.index(0)

    @pl.when(is_end)
    def _():
        for i in range(ahead):
            w_copy(i).start()

    chunk = width // chunks

    def chunk_copy(b, j):
        at = att.at[b, :, pl.ds(j * chunk, chunk)]
        return remote(at, at, a_send.at[j], a_recv.at[j], {"ctx": other})

    def end_copy(r):
        at = att.at[end, pl.ds(r * BLOCK, BLOCK)]
        return remote(at, at, e_send.at[r], e_recv.at[r], {"ctx": my_hub})

    def far_copy(b, r):
        at = att.at[b, pl.ds(r * BLOCK, BLOCK)]
        return remote(at, at, f_send.at[r], f_recv.at[r], {"ctx": other})

    for d in range(1, n):
        pass_on(d, 0)
        if d == 1:
            for p in range(1, pairs):
                pass_on(d, p)
    load_q.wait()

    factor = math.log2(math.e) / HD**0.5
    per_chunk = heads // chunks
    for j in range(chunks):
        if (j * per_chunk) % per_pair == 0:
            p = j * per_chunk // per_pair
            v_ext[:, :HD] = kv_all[:, (2 * p + 1) * HD : (2 * p + 2) * HD]
            if p == 0:
                v_ext[:, HD:] = jnp.ones((v_ext.shape[0], HD), v_ext.dtype)
        p = j * per_chunk // per_pair
        keys_at = pl.ds(2 * p * HD, HD)

        @pl.loop(j * per_chunk, (j + 1) * per_chunk)
        def _(h):
            cols = pl.ds(pl.multiple_of(h * HD, HD), HD)
            keys = kv_all[:, keys_at]
            for start in range(0, tokens, ROWS):
                rows = pl.ds(start, ROWS)
                scores = lax.dot_general(
                    q_ref[rows, cols], keys, (((1,), (1,)), ((), ())), preferred_element_type=jnp.float32
                )
                row_max = jnp.max(scores, axis=1, keepdims=True)
                weights = jnp.exp2((scores - row_max) * factor).astype(jnp.bfloat16)
                both = jnp.dot(weights, v_ext[...], preferred_element_type=jnp.float32)
                att[me, rows, cols] = (both[:, :HD] / both[:, HD:]).astype(att.dtype)

        pl.when(is_hub)(functools.partial(lambda j: chunk_copy(me, j).start(), j))
        if j == 1:
            for d in range(2, n):
                for p in range(1, pairs):
                    pass_on(d, p)
        if j % 2 == 1:
            pl.when(is_hub)(functools.partial(relay_w, j // 2))

    @pl.when(is_end)
    def _():
        i = ahead
        for what in ORDER[ahead:]:
            if what == "w":
                w_copy(i).start()
                i += 1
            else:
                end_copy(what).start()

    late = tiles - EARLY

    def geometry(kind, r):
        if kind == "near":
            return 0, r * BLOCK, BLOCK, 0, tiles, r
        if kind == "early":
            return 1, r * BLOCK, BLOCK, 0, EARLY, blocks + r
        return 1, 0, tokens, r, 1, 2 * blocks + r - EARLY

    def region(kind, r, half=None):
        cb, row, m, c, k, index = geometry(kind, r)
        if half is not None:
            row, m = row + half * (m // 2), m // 2
            row = row if isinstance(row, int) else pl.multiple_of(row, m)
        return cb, pl.ds(row, m), pl.ds(c * tile, k * tile), index

    def product(t, row, m, cb, c, k):
        source = w_far if cb else w

        @pl.loop(c, c + k)
        def _(i):
            cols = pl.ds(pl.multiple_of(i * tile, tile), tile)
            part[t, cb, pl.ds(row, m), cols] = jnp.dot(
                att[t, pl.ds(row, m)], source[:, cols], preferred_element_type=jnp.float32
            ).astype(part.dtype)

    def core_copy(t, kind, r):
        cb, rows, cols, index = region(kind, r)
        return remote(
            part.at[t, cb, rows, cols], rx1.at[t // 2, cb, rows, cols],
            s1.at[t // 2, index], r1.at[t // 2, index], {"sub": away_sub},
        )

    def head_copy(t, kind, r):
        cb, rows, cols, index = region(kind, r, away_head)
        half, short = geometry(kind, r)[1] // 2, geometry(kind, r)[2] // 2
        return remote(
            part.at[t, cb, rows, cols], rx2.at[t // 2, cb, pl.ds(half, short), cols],
            s2.at[t // 2, index], r2.at[t // 2, index], {"head": away_head},
        )

    def is_kept(t, cb):
        if cb:
            return jnp.bool_(False)
        return jnp.logical_and(t == me, keeps)

    def last_copy(t, kind, r):
        cb, rows, cols, index = region(kind, r, head)
        where = {"ctx": t, "head": side, "sub": (me + cb) % 2}
        return remote(
            part.at[t, cb, rows, cols], o_ref.at[rows, cols], s3.at[t // 2, index], r3.at[head, index], where
        )

    def keep_copy(t, kind, r):
        cb, rows, cols, index = region(kind, r, head)
        return pltpu.make_async_copy(part.at[t, cb, rows, cols], o_ref.at[rows, cols], s3.at[t // 2, index])

    def owns(t):
        return t % 2 == sub

    def send(jobs):
        for t, kind, r in jobs:
            pl.when(jnp.logical_not(owns(t)))(functools.partial(lambda *a: core_copy(*a).start(), t, kind, r))

    def multiply(*jobs):
        for t, kind, r in jobs:
            cb, row, m, c, k, _ = geometry(kind, r)
            product(t, row, m, cb, c, k)
            send([(t, kind, r)])

    def multiply_all(t, kind):
        cb, _, _, c, k, _ = geometry(kind, 0)
        product(t, 0, tokens, cb, c, k)
        send([(t, kind, r) for r in range(blocks)])

    def combine(*jobs):
        for t, kind, r in jobs:

            @pl.when(owns(t))
            def _():
                cb, rows, cols, _ = region(kind, r)
                core_copy(t, kind, r).wait_recv()
                total = part[t, cb, rows, cols].astype(jnp.float32)
                total += rx1[t // 2, cb, rows, cols].astype(jnp.float32)
                part[t, cb, rows, cols] = total.astype(part.dtype)
                head_copy(t, kind, r).start()

    def finish(*jobs):
        for t, kind, r in jobs:

            @pl.when(owns(t))
            def _():
                cb, rows, cols, _ = region(kind, r, head)
                half, short = geometry(kind, r)[1] // 2, geometry(kind, r)[2] // 2
                head_copy(t, kind, r).wait_recv()
                total = part[t, cb, rows, cols].astype(jnp.float32)
                total += rx2[t // 2, cb, pl.ds(half, short), cols].astype(jnp.float32)
                part[t, cb, rows, cols] = total.astype(part.dtype)
                if cb:
                    last_copy(t, kind, r).start()
                else:
                    pl.when(is_kept(t, cb))(lambda: keep_copy(t, kind, r).start())
                    pl.when(jnp.logical_not(is_kept(t, cb)))(lambda: last_copy(t, kind, r).start())

    def relay_end(r):
        end_copy(r).wait_recv()
        far_copy(end, r).start()

    def await_far(r):
        far_copy(far_end, r).wait_recv()

    def all_rows(t, kind):
        return [(t, kind, r) for r in range(blocks)]

    def both(t, r):
        return [(t, "near", r), (t, "early", r)]

    @pl.when(is_hub)
    def _():
        g0, g1 = all_rows(me, "near"), all_rows(me, "early")
        g2, g5, g9 = both(end, 0), both(end, 1), both(end, 2)
        g3, g4 = all_rows(other, "near"), all_rows(other, "early")
        g6, g7, g11 = both(far_end, 0), both(far_end, 1), both(far_end, 2)

        def late_of(i, *toks):
            return [(t, "late", i) for t in toks]

        multiply_all(me, "near")
        relay_w(4)
        await_w(0, 1, 2, 3)
        multiply_all(me, "early")
        combine(*g0)
        combine(*g1)
        relay_end(0)
        multiply(*g2)
        finish(*g0)
        finish(*g1)
        combine(*g2)
        for j in range(chunks):
            chunk_copy(other, j).wait_recv()
        multiply_all(other, "near")
        multiply_all(other, "early")
        combine(*g3)
        combine(*g4)
        finish(*g2)
        relay_end(1)
        multiply(*g5)
        await_far(0)
        multiply(*g6)
        combine(*g5)
        finish(*g3)
        finish(*g4)
        combine(*g6)
        relay_w(5)
        finish(*g5)
        relay_w(6)
        finish(*g6)
        await_far(1)
        multiply(*g7)
        await_w(4, 5)
        g8 = late_of(2, me, other)
        multiply(*g8)
        combine(*g7)
        combine(*g8)
        finish(*g7)
        relay_end(2)
        multiply(*g9)
        g9 = g9 + late_of(2, end)
        multiply(*g9[2:])
        finish(*g8)
        combine(*g9)
        relay_w(7)
        finish(*g9)
        relay_w(8)
        await_w(6, 7)
        g10 = late_of(3, me, other, end)
        multiply(*g10)
        await_far(2)
        g11 = g11 + late_of(2, far_end) + late_of(3, far_end)
        multiply(*g11)
        combine(*g10)
        combine(*g11)
        relay_w(9)
        finish(*g10)
        finish(*g11)
        await_w(8, 9)
        g13 = late_of(4, far_end, other, end, me)
        multiply(*g13)
        combine(*g13)
        finish(*g13)

    my_cb = (sub + 1 + head) % 2

    def arrivals(cb):
        kinds = [("near", r) for r in range(blocks)]
        if cb:
            kinds = [("early", r) for r in range(blocks)] + [("late", r) for r in range(EARLY, tiles)]
        for kind, r in kinds:
            for h in range(n_head):
                cb_, rows, cols, index = region(kind, r, h)
                got = remote(
                    part.at[0, cb_, rows, cols], o_ref.at[rows, cols], s3.at[0, index], r3.at[h, index],
                    {"ctx": origin, "head": h, "sub": me % 2},
                )
                if cb:
                    got.wait_recv()
                else:
                    pl.when(jnp.logical_not(jnp.logical_and(mine, head == h)))(lambda: got.wait_recv())

    pl.when(my_cb == 0)(lambda: arrivals(0))
    pl.when(my_cb == 1)(lambda: arrivals(1))

    for way, go in ((0, to_right), (1, to_left)):
        for d in range(n):
            b = me - d if way == 0 else me + d
            fits = b >= 0 if way == 0 else b < n

            @pl.when(jnp.logical_and(fits, go))
            def _():
                for p in range(pairs):
                    kv_copy(b, way, d, p).wait_send()

    @pl.when(is_end)
    def _():
        for i in range(pieces):
            w_copy(i).wait_send()
        for r in range(blocks):
            end_copy(r).wait_send()

    @pl.when(is_hub)
    def _():
        for i in range(pieces):
            y_copy(group, i).wait_send()
        for j in range(chunks):
            chunk_copy(me, j).wait_send()
        for r in range(blocks):
            far_copy(end, r).wait_send()
        names = [("near", r) for r in range(blocks)] + [("early", r) for r in range(blocks)]
        names += [("late", r) for r in range(EARLY, tiles)]
        for t in (me, other, end, far_end):
            for kind, r in names:

                @pl.when(owns(t))
                def _():
                    head_copy(t, kind, r).wait_send()
                    if kind == "near":
                        kept = is_kept(t, 0)
                        pl.when(kept)(lambda: keep_copy(t, kind, r).wait())
                        pl.when(jnp.logical_not(kept))(lambda: last_copy(t, kind, r).wait_send())
                    else:
                        last_copy(t, kind, r).wait_send()

                @pl.when(jnp.logical_not(owns(t)))
                def _():
                    core_copy(t, kind, r).wait_send()


def with_hubs(queries, key_rows, value_rows, out_weight):
    tokens, width = queries.shape
    heads_here = width // HD
    pairs = heads_here // (QH // KVH)
    per_pair = heads_here // pairs
    n = lax.axis_size("ctx")
    n_head = lax.axis_size("head")
    columns = out_weight.shape[1]
    block = (tokens, columns)
    tiles = columns // TILE
    pieces = 2 * tiles
    blocks = tokens // BLOCK
    kinds = 2 * blocks + tiles - EARLY
    anywhere = pl.BlockSpec(memory_space=pl.ANY)
    dma = pltpu.SemaphoreType.DMA
    bf16 = jnp.bfloat16
    sums = [dma((n // 2, kinds))] * 5 + [dma((n_head, kinds))]
    return pl.pallas_call(
        functools.partial(hub_kernel, n, n_head, per_pair, pairs, CHUNKS, TILE),
        out_shape=jax.ShapeDtypeStruct(block, bf16),
        in_specs=[anywhere] * 4,
        out_specs=anywhere,
        scratch_shapes=[
            pltpu.VMEM((n * tokens, 2 * pairs * HD), bf16),
            pltpu.VMEM((n * tokens, 2 * HD), bf16),
            pltpu.VMEM((tokens, width), bf16),
            pltpu.VMEM((n, tokens, width), bf16),
            pltpu.VMEM(out_weight.shape, bf16),
            pltpu.VMEM(out_weight.shape, bf16),
            pltpu.VMEM((n, 2) + block, bf16),
            pltpu.VMEM((n // 2, 2) + block, bf16),
            pltpu.VMEM((n // 2, 2, tokens // 2, columns), bf16),
            dma((2 * pairs + 2,)),
            dma((2, n, pairs)),
            dma((n, pairs)),
            dma((CHUNKS,)),
            dma((CHUNKS,)),
            dma((blocks,)),
            dma((blocks,)),
            dma((blocks,)),
            dma((blocks,)),
            dma((pieces,)),
            dma((pieces,)),
            dma((pieces,)),
            dma((pieces,)),
        ] + sums,
        compiler_params=pltpu.CompilerParams(
            collective_id=0, has_side_effects=True, vmem_limit_bytes=60 * 2**20
        ),
    )(key_rows, value_rows, queries, out_weight)


def hubs_fit(mesh, queries, out_weight):
    shape = mesh.shape
    tokens, width = queries[0] // (shape["groups"] * shape["ctx"]), queries[1] // (shape["head"] * shape["sub"])
    columns = out_weight[1] // shape["ctx"]
    sizes = (shape["groups"], shape["ctx"], shape["head"], shape["sub"]) == (2, 4, 2, 2)
    heads = width // HD
    return sizes and tokens == 3 * BLOCK and columns == 5 * TILE and heads == 2 * CHUNKS and heads * KVH == 2 * QH


def solution(mesh):
    assert mesh.shape["sub"] == 2
    assert mesh.shape["ctx"] == mesh.shape["head"] * mesh.shape["sub"]

    def run(queries, key_rows, value_rows, out_weight):
        fits = hubs_fit(mesh, queries.shape, out_weight.shape)
        return jax.shard_map(
            with_hubs if fits else on_device,
            mesh=mesh,
            in_specs=(
                P(("groups", "ctx"), ("head", "sub")),
                P(("groups", "ctx"), "head"),
                P(("groups", "ctx"), "head"),
                P(("head", "sub"), "ctx"),
            ),
            out_specs=P(("groups", "ctx"), ("head", "sub")),
            check_vma=False,
        )(queries, key_rows, value_rows, out_weight)

    return run
```

```python
import functools
import math

import jax
import jax.numpy as jnp
from jax import lax
from jax.experimental import pallas as pl
from jax.experimental.pallas import tpu as pltpu
from jax.sharding import PartitionSpec as P

QH = 64
KVH = 8
HD = 128
CHUNKS = 8
TILE = 256
ROWS = 128
MESH = pl.DeviceIdType.MESH
BLOCK = 128
EARLY = 2
SPLIT = 4
TOGETHER = 4
ORDER = ("w",) * 8 + (0, 1, 2) + ("w",) * 12


def kernel(
    n, n_head, per_pair, pairs, chunks, parts, k_hbm, v_hbm, q_hbm, w_hbm, o_ref,
    kv_all, v_ext, q_ref, att, w, own, out, rx1, summed, rx2, final,
    load_sems, kv_send, kv_recv, a_send, a_recv, s1, r1, s2, r2, s3, r3,
):
    me, head, sub = (lax.axis_index(a) for a in ("ctx", "head", "sub"))
    other = 1 - sub
    hs = head * 2 + sub
    tokens, width = q_ref.shape
    heads = width // HD
    columns = w.shape[1]
    piece = width // chunks
    to_right, to_left = me < n - 1, me > 0
    right, left = lax.min(me + 1, n - 1), lax.max(me - 1, 0)
    away = hs != me
    share = tokens // n_head

    def rows_of(b):
        return pl.ds(pl.multiple_of(b * tokens, tokens), tokens)

    first = pl.multiple_of((sub * heads // (QH // KVH)) * HD, HD)
    loads = [
        pltpu.make_async_copy(
            side.at[:, pl.ds(first, pairs * HD)],
            kv_all.at[rows_of(me), pl.ds(i * pairs * HD, pairs * HD)],
            load_sems.at[i],
        )
        for i, side in enumerate((k_hbm, v_hbm))
    ]
    loads.append(pltpu.make_async_copy(q_hbm, q_ref, load_sems.at[2]))
    loads.append(pltpu.make_async_copy(w_hbm, w, load_sems.at[3]))
    for load in loads:
        load.start()

    barrier = pltpu.get_barrier_semaphore()

    def greet(where):
        pl.semaphore_signal(barrier, inc=1, device_id=where, device_id_type=MESH)

    pl.when(to_right)(lambda: greet({"ctx": right}))
    pl.when(to_left)(lambda: greet({"ctx": left}))
    for h in range(n_head):
        source = {"ctx": hs, "head": h, "sub": me % 2}
        pl.when(jnp.logical_or(away, head != h))(functools.partial(greet, source))
    greet({"sub": other})
    for step in range(1, n_head):
        greet({"head": lax.rem(head + step, n_head)})
    count = 2 * n_head - 1 + to_right.astype(jnp.int32) + to_left.astype(jnp.int32)
    pl.semaphore_wait(barrier, count + away.astype(jnp.int32))

    def remote(src, dst, send, recv, where):
        return pltpu.make_async_remote_copy(
            src_ref=src, dst_ref=dst, send_sem=send, recv_sem=recv, device_id=where, device_id_type=MESH
        )

    def kv_copy(b, way, d):
        where = {"ctx": right if way == 0 else left}
        part = kv_all.at[rows_of(b)]
        return remote(part, part, kv_send.at[way, d], kv_recv.at[b], where)

    loads[0].wait()
    loads[1].wait()
    pl.when(to_right)(lambda: kv_copy(me, 0, 0).start())
    pl.when(to_left)(lambda: kv_copy(me, 1, 0).start())

    @pl.loop(1, n)
    def _(d):
        @pl.when(me - d >= 0)
        def _():
            copy = kv_copy(me - d, 0, d)
            copy.wait_recv()
            pl.when(to_right)(lambda: copy.start())

        @pl.when(me + d < n)
        def _():
            copy = kv_copy(me + d, 1, d)
            copy.wait_recv()
            pl.when(to_left)(lambda: copy.start())

    loads[2].wait()

    def a_copy(b, j, way, d):
        where = {"ctx": right if way == 0 else left}
        part = att.at[b, :, pl.ds(j * piece, piece)]
        return remote(part, part, a_send.at[way, d, j], a_recv.at[b, j], where)

    factor = math.log2(math.e) / HD**0.5
    for j in range(chunks):
        if j % (chunks // pairs) == 0:
            p = j // (chunks // pairs)
            v_ext[p, :, :HD] = kv_all[:, (pairs + p) * HD : (pairs + p + 1) * HD]
            v_ext[p, :, HD:] = jnp.ones((v_ext.shape[1], HD), v_ext.dtype)

        @pl.loop(j * heads // chunks, (j + 1) * heads // chunks)
        def _(h):
            pair = h // per_pair
            cols = pl.ds(pl.multiple_of(h * HD, HD), HD)
            keys = kv_all[:, pl.ds(pl.multiple_of(pair * HD, HD), HD)]
            for start in range(0, tokens, ROWS):
                rows = pl.ds(start, ROWS)
                scores = lax.dot_general(
                    q_ref[rows, cols], keys, (((1,), (1,)), ((), ())), preferred_element_type=jnp.float32
                )
                row_max = jnp.max(scores, axis=1, keepdims=True)
                weights = jnp.exp2((scores - row_max) * factor).astype(jnp.bfloat16)
                both = jnp.dot(weights, v_ext[pair], preferred_element_type=jnp.float32)
                att[me, rows, cols] = (both[:, :HD] / both[:, HD:]).astype(att.dtype)

        pl.when(to_right)(lambda: a_copy(me, j, 0, 0).start())
        pl.when(to_left)(lambda: a_copy(me, j, 1, 0).start())

    loads[3].wait()
    tile = columns // parts

    def cols_of(c):
        return pl.ds(0, columns) if parts == 1 else pl.ds(pl.multiple_of(c * tile, tile), tile)

    def core_copy(g, c):
        cols = cols_of(c)
        return remote(out.at[g, :, cols], rx1.at[g, :, cols], s1.at[g, c], r1.at[g, c], {"sub": other})

    def share_of(h):
        return pl.ds(pl.multiple_of(h * share, share), share)

    def head_copy(g, step, c):
        cols, target = cols_of(c), lax.rem(head + step, n_head)
        return remote(
            summed.at[g, share_of(target), cols], rx2.at[g, head, :, cols],
            s2.at[g, step - 1, c], r2.at[g, head, c], {"head": target},
        )

    def head_arrival(g, source, c):
        cols = cols_of(c)
        return remote(
            summed.at[g, share_of(source), cols], rx2.at[g, source, :, cols],
            s2.at[g, 0, c], r2.at[g, source, c], {"head": source},
        )

    def last_copy(g, h, c):
        cols = cols_of(c)
        where = {"ctx": 2 * g + sub, "head": me // 2, "sub": me % 2}
        return remote(final.at[g, :, cols], o_ref.at[share_of(h), cols], s3.at[g, c], r3.at[h, c], where)

    def product(t, c):
        cols = cols_of(c)
        return jnp.dot(att[t], w[:, cols], preferred_element_type=jnp.float32).astype(out.dtype)

    def multiply(t):
        g = t // 2

        @pl.when(t % 2 == sub)
        def _():
            @pl.loop(0, parts)
            def _(c):
                own[g, :, cols_of(c)] = product(t, c)

        @pl.when(t % 2 != sub)
        def _():
            @pl.loop(0, parts)
            def _(c):
                out[g, :, cols_of(c)] = product(t, c)
                core_copy(g, c).start()

    def combine(t):
        g = t // 2

        @pl.when(t % 2 == sub)
        def _():
            @pl.loop(0, parts)
            def _(c):
                cols = cols_of(c)
                core_copy(g, c).wait_recv()
                total = own[g, :, cols].astype(jnp.float32) + rx1[g, :, cols].astype(jnp.float32)
                summed[g, :, cols] = total.astype(summed.dtype)
                for step in range(1, n_head):
                    head_copy(g, step, c).start()

    def finish(t):
        g = t // 2

        @pl.when(t % 2 == sub)
        def _():
            @pl.loop(0, parts)
            def _(c):
                cols = cols_of(c)
                total = summed[g, share_of(head), cols].astype(jnp.float32)
                for step in range(1, n_head):
                    source = lax.rem(head + step, n_head)
                    head_arrival(g, source, c).wait_recv()
                    total += rx2[g, source, :, cols].astype(jnp.float32)
                final[g, :, cols] = total.astype(final.dtype)
                pl.when(jnp.logical_or(away, t != me))(lambda: last_copy(g, head, c).start())

    def finish_at(d):
        pl.when(jnp.logical_and(d >= 0, me - d >= 0))(lambda: finish(me - d))
        pl.when(jnp.logical_and(d > 0, me + d < n))(lambda: finish(me + d))

    def after(d, j, last=False):
        behind, ahead = me - d + 1, me + d - 1
        if j == 0:
            pl.when(behind >= 0)(lambda: multiply(behind))
        if j == chunks // 4:
            pl.when(jnp.logical_and(ahead < n, d > 1))(lambda: multiply(ahead))
        if j == chunks // 2:
            pl.when(behind >= 0)(lambda: combine(behind))
        if j == chunks // 2 + 1:
            pl.when(jnp.logical_and(ahead < n, d > 1))(lambda: combine(ahead))
        if j == chunks - 1 and not last:
            finish_at(d - 2)

    @pl.loop(1, n)
    def _(d):
        for j in range(chunks):

            @pl.when(me - d >= 0)
            def _():
                copy = a_copy(me - d, j, 0, d)
                copy.wait_recv()
                pl.when(to_right)(lambda: copy.start())

            @pl.when(me + d < n)
            def _():
                copy = a_copy(me + d, j, 1, d)
                copy.wait_recv()
                pl.when(to_left)(lambda: copy.start())

            after(d, j)

    finish_at(n - 2)
    for j in range(chunks):
        after(n, j, last=True)
    finish_at(n - 1)

    @pl.when(jnp.logical_not(away))
    def _():
        keep = pltpu.make_async_copy(final.at[me // 2], o_ref.at[share_of(head)], load_sems.at[0])
        keep.start()
        keep.wait()

    for h in range(n_head):

        @pl.when(jnp.logical_or(away, head != h))
        def _():
            @pl.loop(0, parts)
            def _(c):
                last_copy(0, h, c).wait_recv()

    @pl.loop(0, n)
    def _(d):
        for way, fits, go in ((0, me - d >= 0, to_right), (1, me + d < n, to_left)):
            b = me - d if way == 0 else me + d

            @pl.when(jnp.logical_and(fits, go))
            def _():
                kv_copy(b, way, d).wait_send()
                for j in range(chunks):
                    a_copy(b, j, way, d).wait_send()

    @pl.loop(0, n // 2)
    def _(g):
        @pl.loop(0, parts)
        def _(c):
            core_copy(g, c).wait_send()
            for step in range(1, n_head):
                head_copy(g, step, c).wait_send()
            pl.when(jnp.logical_or(away, 2 * g + sub != me))(lambda: last_copy(g, head, c).wait_send())


def on_device(queries, key_rows, value_rows, out_weight):
    tokens, width = queries.shape
    heads_here = width // HD
    group_ratio = QH // KVH
    pairs = max(heads_here // group_ratio, 1)
    per_pair = heads_here // pairs
    n = lax.axis_size("ctx")
    n_head = lax.axis_size("head")
    columns = out_weight.shape[1]
    block = (tokens, columns)
    groups = (n // 2,) + block
    chunks = min(CHUNKS, heads_here)
    parts = columns // TILE if columns % TILE == 0 else 1
    anywhere = pl.BlockSpec(memory_space=pl.ANY)
    dma = pltpu.SemaphoreType.DMA
    bf16 = jnp.bfloat16
    return pl.pallas_call(
        functools.partial(kernel, n, n_head, per_pair, pairs, chunks, parts),
        out_shape=jax.ShapeDtypeStruct(block, bf16),
        in_specs=[anywhere] * 4,
        out_specs=anywhere,
        scratch_shapes=[
            pltpu.VMEM((n * tokens, 2 * pairs * HD), bf16),
            pltpu.VMEM((pairs, n * tokens, 2 * HD), bf16),
            pltpu.VMEM((tokens, width), bf16),
            pltpu.VMEM((n, tokens, width), bf16),
            pltpu.VMEM(out_weight.shape, bf16),
            pltpu.VMEM(groups, bf16),
            pltpu.VMEM(groups, bf16),
            pltpu.VMEM(groups, bf16),
            pltpu.VMEM(groups, bf16),
            pltpu.VMEM((n // 2, n_head, tokens // n_head, columns), bf16),
            pltpu.VMEM((n // 2, tokens // n_head, columns), bf16),
            dma((4,)),
            dma((2, n)),
            dma((n,)),
            dma((2, n, chunks)),
            dma((n, chunks)),
            dma((n // 2, parts)),
            dma((n // 2, parts)),
            dma((n // 2, n_head - 1, parts)),
            dma((n // 2, n_head, parts)),
            dma((n // 2, parts)),
            dma((n_head, parts)),
        ],
        compiler_params=pltpu.CompilerParams(
            collective_id=0, has_side_effects=True, vmem_limit_bytes=60 * 2**20
        ),
    )(key_rows, value_rows, queries, out_weight)


def hub_kernel(
    n, n_head, per_pair, pairs, chunks, tile, k_hbm, v_hbm, q_hbm, w_hbm, o_ref,
    kv_all, v_ext, q_ref, att, w, w_far, part, rx1, rx2,
    load_sems, kv_send, kv_recv, a_send, a_recv, e_send, e_recv, f_send, f_recv,
    w_send, w_recv, y_send, y_recv, s1, r1, s2, r2, s3, r3,
):
    me, head, sub, group = (lax.axis_index(a) for a in ("ctx", "head", "sub", "groups"))
    tokens, width = q_ref.shape
    heads = width // HD
    columns = w.shape[1]
    blocks = tokens // BLOCK
    tiles = columns // tile
    pieces = SPLIT * tiles
    per_piece = width // (2 * SPLIT)
    low = n // 2 - 1
    is_hub = jnp.logical_and(me >= low, me <= low + 1)
    is_end = jnp.logical_not(is_hub)
    to_right, to_left = me < n - 1, me > 0
    right, left = lax.min(me + 1, n - 1), lax.max(me - 1, 0)
    other = n - 1 - me
    end = jnp.where(me <= low, 0, n - 1)
    far_end = n - 1 - end
    my_hub = jnp.where(me <= low, low, low + 1)
    side = me - low
    away_head, away_sub, away_group = 1 - head, 1 - sub, 1 - group

    def rows_of(b):
        return pl.ds(pl.multiple_of(b * tokens, tokens), tokens)

    first = pl.multiple_of((sub * heads // (QH // KVH)) * HD, HD)
    loads = []
    for p in range(pairs):
        for i, ref in enumerate((k_hbm, v_hbm)):
            loads.append(pltpu.make_async_copy(
                ref.at[:, pl.ds(pl.multiple_of(first + p * HD, HD), HD)],
                kv_all.at[rows_of(me), pl.ds((2 * p + i) * HD, HD)],
                load_sems.at[2 * p + i],
            ))
    load_w = pltpu.make_async_copy(w_hbm, w, load_sems.at[2 * pairs])
    load_q = pltpu.make_async_copy(q_hbm, q_ref, load_sems.at[2 * pairs + 1])
    for load in loads + [load_w, load_q]:
        load.start()

    barrier = pltpu.get_barrier_semaphore()

    def greet(where):
        pl.semaphore_signal(barrier, inc=1, device_id=where, device_id_type=MESH)

    pl.when(to_right)(lambda: greet({"ctx": right}))
    pl.when(to_left)(lambda: greet({"ctx": left}))
    greet({"sub": away_sub})
    greet({"head": away_head})
    greet({"groups": away_group})
    origin = low + head
    mine = jnp.logical_and(me == origin, sub == me % 2)
    for h in range(n_head):
        source = {"ctx": origin, "head": h, "sub": me % 2}
        pl.when(jnp.logical_not(jnp.logical_and(mine, head == h)))(functools.partial(greet, source))
    keeps = jnp.logical_and(is_hub, jnp.logical_and(head == side, sub == me % 2))
    count = 3 + to_right.astype(jnp.int32) + to_left.astype(jnp.int32)
    count += jnp.where(is_hub, 4, 0) - keeps.astype(jnp.int32)
    pl.semaphore_wait(barrier, count)

    def remote(src, dst, send, recv, where):
        return pltpu.make_async_remote_copy(
            src_ref=src, dst_ref=dst, send_sem=send, recv_sem=recv, device_id=where, device_id_type=MESH
        )

    def kv_copy(b, way, d, p):
        where = {"ctx": right if way == 0 else left}
        block = kv_all.at[rows_of(b), pl.ds(2 * p * HD, 2 * HD)]
        return remote(block, block, kv_send.at[way, d, p], kv_recv.at[b, p], where)

    for p in range(pairs):
        loads[2 * p].wait()
        loads[2 * p + 1].wait()
        pl.when(to_right)(lambda: kv_copy(me, 0, 0, p).start())
        pl.when(to_left)(lambda: kv_copy(me, 1, 0, p).start())

    def pass_on(d, p):
        @pl.when(me - d >= 0)
        def _():
            copy = kv_copy(me - d, 0, d, p)
            copy.wait_recv()
            pl.when(to_right)(lambda: copy.start())

        @pl.when(me + d < n)
        def _():
            copy = kv_copy(me + d, 1, d, p)
            copy.wait_recv()
            pl.when(to_left)(lambda: copy.start())

    def w_piece(g, i):
        rows = pl.ds(pl.multiple_of(g * (width // 2) + (i % SPLIT) * per_piece, per_piece), per_piece)
        return rows, pl.ds((i // SPLIT) * tile, tile)

    def w_copy(i):
        at = w_piece(group, i)
        return remote(w.at[at], w_far.at[at], w_send.at[i], w_recv.at[i], {"ctx": my_hub})

    def y_copy(g, i):
        at = w_piece(g, i)
        return remote(w_far.at[at], w_far.at[at], y_send.at[i], y_recv.at[i], {"groups": away_group})

    def relay_w(*which):
        for i in which:
            w_copy(i).wait_recv()
            y_copy(group, i).start()

    def await_w(*which):
        for i in which:
            y_copy(away_group, i).wait_recv()

    load_w.wait()
    ahead = ORDER.index(0)

    @pl.when(is_end)
    def _():
        for i in range(ahead):
            w_copy(i).start()

    chunk = width // chunks

    def chunk_copy(b, j):
        at = att.at[b, :, pl.ds(j * chunk, chunk)]
        return remote(at, at, a_send.at[j], a_recv.at[j], {"ctx": other})

    def end_copy(r):
        at = att.at[end, pl.ds(r * BLOCK, BLOCK)]
        return remote(at, at, e_send.at[r], e_recv.at[r], {"ctx": my_hub})

    def far_copy(b, r):
        at = att.at[b, pl.ds(r * BLOCK, BLOCK)]
        return remote(at, at, f_send.at[r], f_recv.at[r], {"ctx": other})

    for d in range(1, n):
        pass_on(d, 0)
        if d == 1:
            for p in range(1, pairs):
                pass_on(d, p)
    load_q.wait()

    factor = math.log2(math.e) / HD**0.5
    per_chunk = heads // chunks

    def prepare(p):
        v_ext[p, :, :HD] = kv_all[:, (2 * p + 1) * HD : (2 * p + 2) * HD]
        v_ext[p, :, HD:] = jnp.ones((v_ext.shape[1], HD), v_ext.dtype)

    def attend(h, p, start):
        rows, cols = pl.ds(start, ROWS), pl.ds(pl.multiple_of(h * HD, HD), HD)
        keys = kv_all[:, 2 * p * HD : (2 * p + 1) * HD]
        scores = lax.dot_general(
            q_ref[rows, cols], keys, (((1,), (1,)), ((), ())), preferred_element_type=jnp.float32
        )
        row_max = jnp.max(scores, axis=1, keepdims=True)
        weights = jnp.exp2((scores - row_max) * factor).astype(jnp.bfloat16)
        both = jnp.dot(weights, v_ext[p], preferred_element_type=jnp.float32)
        att[me, rows, cols] = (both[:, :HD] / both[:, HD:]).astype(att.dtype)

    def rest_of_pairs():
        for d in range(2, n):
            for p in range(1, pairs):
                pass_on(d, p)

    @pl.when(is_hub)
    def _():
        relay_w(0)
        for j in range(chunks):
            p = j * per_chunk // per_pair
            if (j * per_chunk) % per_pair == 0:
                prepare(p)

            @pl.loop(j * per_chunk, (j + 1) * per_chunk)
            def _(h):
                for start in range(0, tokens, ROWS):
                    attend(h, p, start)

            chunk_copy(me, j).start()
            if j == 1:
                rest_of_pairs()
            if j + 1 < chunks:
                relay_w(j + 1)

    @pl.when(is_end)
    def _():
        i = ahead
        prepare(0)
        for r in range(blocks):
            for p in range(pairs):
                if r == 0 and p == 1:
                    rest_of_pairs()
                    for q in range(1, pairs):
                        prepare(q)

                @pl.loop(p * per_pair, (p + 1) * per_pair, step=TOGETHER)
                def _(h):
                    for k in range(TOGETHER):
                        for start in range(r * BLOCK, (r + 1) * BLOCK, ROWS):
                            attend(h + k, p, start)

            end_copy(r).start()
            after = ORDER.index(r) + 1
            while after < len(ORDER) and ORDER[after] == "w":
                w_copy(i).start()
                i, after = i + 1, after + 1

    late = tiles - EARLY

    def geometry(kind, r):
        if kind == "near":
            return 0, r * BLOCK, BLOCK, 0, tiles, r
        if kind == "early":
            return 1, r * BLOCK, BLOCK, 0, EARLY, blocks + r
        return 1, 0, tokens, r, 1, 2 * blocks + r - EARLY

    def region(kind, r, half=None):
        cb, row, m, c, k, index = geometry(kind, r)
        if half is not None:
            row, m = row + half * (m // 2), m // 2
            row = row if isinstance(row, int) else pl.multiple_of(row, m)
        return cb, pl.ds(row, m), pl.ds(c * tile, k * tile), index

    def product(t, row, m, cb, c, k):
        source = w_far if cb else w

        @pl.loop(c, c + k)
        def _(i):
            cols = pl.ds(pl.multiple_of(i * tile, tile), tile)
            part[t, cb, pl.ds(row, m), cols] = jnp.dot(
                att[t, pl.ds(row, m)], source[:, cols], preferred_element_type=jnp.float32
            ).astype(part.dtype)

    def core_copy(t, kind, r):
        cb, rows, cols, index = region(kind, r)
        return remote(
            part.at[t, cb, rows, cols], rx1.at[t // 2, cb, rows, cols],
            s1.at[t // 2, index], r1.at[t // 2, index], {"sub": away_sub},
        )

    def head_copy(t, kind, r):
        cb, rows, cols, index = region(kind, r, away_head)
        half, short = geometry(kind, r)[1] // 2, geometry(kind, r)[2] // 2
        return remote(
            part.at[t, cb, rows, cols], rx2.at[t // 2, cb, pl.ds(half, short), cols],
            s2.at[t // 2, index], r2.at[t // 2, index], {"head": away_head},
        )

    def is_kept(t, cb):
        if cb:
            return jnp.bool_(False)
        return jnp.logical_and(t == me, keeps)

    def last_copy(t, kind, r):
        cb, rows, cols, index = region(kind, r, head)
        where = {"ctx": t, "head": side, "sub": (me + cb) % 2}
        return remote(
            part.at[t, cb, rows, cols], o_ref.at[rows, cols], s3.at[t // 2, index], r3.at[head, index], where
        )

    def keep_copy(t, kind, r):
        cb, rows, cols, index = region(kind, r, head)
        return pltpu.make_async_copy(part.at[t, cb, rows, cols], o_ref.at[rows, cols], s3.at[t // 2, index])

    def owns(t):
        return t % 2 == sub

    def send(jobs):
        for t, kind, r in jobs:
            pl.when(jnp.logical_not(owns(t)))(functools.partial(lambda *a: core_copy(*a).start(), t, kind, r))

    def multiply(*jobs):
        for t, kind, r in jobs:
            cb, row, m, c, k, _ = geometry(kind, r)
            product(t, row, m, cb, c, k)
            send([(t, kind, r)])

    def multiply_all(t, kind):
        cb, _, _, c, k, _ = geometry(kind, 0)
        product(t, 0, tokens, cb, c, k)
        send([(t, kind, r) for r in range(blocks)])

    def combine(*jobs):
        for t, kind, r in jobs:

            @pl.when(owns(t))
            def _():
                cb, rows, cols, _ = region(kind, r)
                core_copy(t, kind, r).wait_recv()
                total = part[t, cb, rows, cols].astype(jnp.float32)
                total += rx1[t // 2, cb, rows, cols].astype(jnp.float32)
                part[t, cb, rows, cols] = total.astype(part.dtype)
                head_copy(t, kind, r).start()

    def finish(*jobs):
        for t, kind, r in jobs:

            @pl.when(owns(t))
            def _():
                cb, rows, cols, _ = region(kind, r, head)
                half, short = geometry(kind, r)[1] // 2, geometry(kind, r)[2] // 2
                head_copy(t, kind, r).wait_recv()
                total = part[t, cb, rows, cols].astype(jnp.float32)
                total += rx2[t // 2, cb, pl.ds(half, short), cols].astype(jnp.float32)
                part[t, cb, rows, cols] = total.astype(part.dtype)
                if cb:
                    last_copy(t, kind, r).start()
                else:
                    pl.when(is_kept(t, cb))(lambda: keep_copy(t, kind, r).start())
                    pl.when(jnp.logical_not(is_kept(t, cb)))(lambda: last_copy(t, kind, r).start())

    def relay_end(r):
        end_copy(r).wait_recv()
        far_copy(end, r).start()

    def await_far(r):
        far_copy(far_end, r).wait_recv()

    def all_rows(t, kind):
        return [(t, kind, r) for r in range(blocks)]

    def both(t, r):
        return [(t, "near", r), (t, "early", r)]

    @pl.when(is_hub)
    def _():
        g0, g1 = all_rows(me, "near"), all_rows(me, "early")
        g2, g5, g9 = both(end, 0), both(end, 1), both(end, 2)
        g3, g4 = all_rows(other, "near"), all_rows(other, "early")
        g6, g7, g11 = both(far_end, 0), both(far_end, 1), both(far_end, 2)

        def late_of(i, *toks):
            return [(t, "late", i) for t in toks]

        g8, g10 = late_of(2, me, other, end), late_of(3, far_end, other, end, me)
        g11 = g11 + late_of(2, far_end)
        g12, g13 = late_of(4, far_end, other), late_of(4, end, me)

        multiply_all(me, "near")
        await_w(*range(8))
        multiply_all(me, "early")
        combine(*g0)
        combine(*g1)
        relay_end(0)
        multiply(*g2)
        combine(*g2)
        finish(*g0)
        finish(*g1)
        for j in range(chunks):
            chunk_copy(other, j).wait_recv()
        multiply_all(other, "near")
        relay_end(1)
        multiply_all(other, "early")
        combine(*g3)
        combine(*g4)
        multiply(*g5)
        finish(*g2)
        combine(*g5)
        await_far(0)
        multiply(*g6)
        relay_end(2)
        combine(*g6)
        multiply(*g9)
        relay_w(8)
        combine(*g9)
        finish(*g3)
        relay_w(9)
        finish(*g4)
        relay_w(10)
        finish(*g5)
        await_far(1)
        multiply(*g7)
        relay_w(11)
        combine(*g7)
        finish(*g6)
        relay_w(12)
        await_w(8, 9, 10, 11)
        multiply(*g8)
        relay_w(13)
        combine(*g8)
        finish(*g9)
        await_far(2)
        relay_w(14)
        multiply(*g11)
        relay_w(15)
        combine(*g11)
        finish(*g7)
        relay_w(16)
        await_w(12, 13, 14, 15)
        multiply(*g10[:2])
        relay_w(17)
        multiply(*g10[2:])
        relay_w(18)
        combine(*g10)
        finish(*g8)
        finish(*g11)
        relay_w(19)
        finish(*g10)
        await_w(16, 17, 18, 19)
        multiply(*g12)
        combine(*g12)
        multiply(*g13)
        combine(*g13)
        finish(*g12)
        finish(*g13)

    my_cb = (sub + 1 + head) % 2

    def arrivals(cb):
        kinds = [("near", r) for r in range(blocks)]
        if cb:
            kinds = [("early", r) for r in range(blocks)] + [("late", r) for r in range(EARLY, tiles)]
        for kind, r in kinds:
            for h in range(n_head):
                cb_, rows, cols, index = region(kind, r, h)
                got = remote(
                    part.at[0, cb_, rows, cols], o_ref.at[rows, cols], s3.at[0, index], r3.at[h, index],
                    {"ctx": origin, "head": h, "sub": me % 2},
                )
                if cb:
                    got.wait_recv()
                else:
                    pl.when(jnp.logical_not(jnp.logical_and(mine, head == h)))(lambda: got.wait_recv())

    pl.when(my_cb == 0)(lambda: arrivals(0))
    pl.when(my_cb == 1)(lambda: arrivals(1))

    for way, go in ((0, to_right), (1, to_left)):
        for d in range(n):
            b = me - d if way == 0 else me + d
            fits = b >= 0 if way == 0 else b < n

            @pl.when(jnp.logical_and(fits, go))
            def _():
                for p in range(pairs):
                    kv_copy(b, way, d, p).wait_send()

    @pl.when(is_end)
    def _():
        for i in range(pieces):
            w_copy(i).wait_send()
        for r in range(blocks):
            end_copy(r).wait_send()

    @pl.when(is_hub)
    def _():
        for i in range(pieces):
            y_copy(group, i).wait_send()
        for j in range(chunks):
            chunk_copy(me, j).wait_send()
        for r in range(blocks):
            far_copy(end, r).wait_send()
        names = [("near", r) for r in range(blocks)] + [("early", r) for r in range(blocks)]
        names += [("late", r) for r in range(EARLY, tiles)]
        for t in (me, other, end, far_end):
            for kind, r in names:

                @pl.when(owns(t))
                def _():
                    head_copy(t, kind, r).wait_send()
                    if kind == "near":
                        kept = is_kept(t, 0)
                        pl.when(kept)(lambda: keep_copy(t, kind, r).wait())
                        pl.when(jnp.logical_not(kept))(lambda: last_copy(t, kind, r).wait_send())
                    else:
                        last_copy(t, kind, r).wait_send()

                @pl.when(jnp.logical_not(owns(t)))
                def _():
                    core_copy(t, kind, r).wait_send()


def with_hubs(queries, key_rows, value_rows, out_weight):
    tokens, width = queries.shape
    heads_here = width // HD
    pairs = heads_here // (QH // KVH)
    per_pair = heads_here // pairs
    n = lax.axis_size("ctx")
    n_head = lax.axis_size("head")
    columns = out_weight.shape[1]
    block = (tokens, columns)
    tiles = columns // TILE
    pieces = SPLIT * tiles
    blocks = tokens // BLOCK
    kinds = 2 * blocks + tiles - EARLY
    anywhere = pl.BlockSpec(memory_space=pl.ANY)
    dma = pltpu.SemaphoreType.DMA
    bf16 = jnp.bfloat16
    sums = [dma((n // 2, kinds))] * 5 + [dma((n_head, kinds))]
    return pl.pallas_call(
        functools.partial(hub_kernel, n, n_head, per_pair, pairs, CHUNKS, TILE),
        out_shape=jax.ShapeDtypeStruct(block, bf16),
        in_specs=[anywhere] * 4,
        out_specs=anywhere,
        scratch_shapes=[
            pltpu.VMEM((n * tokens, 2 * pairs * HD), bf16),
            pltpu.VMEM((pairs, n * tokens, 2 * HD), bf16),
            pltpu.VMEM((tokens, width), bf16),
            pltpu.VMEM((n, tokens, width), bf16),
            pltpu.VMEM(out_weight.shape, bf16),
            pltpu.VMEM(out_weight.shape, bf16),
            pltpu.VMEM((n, 2) + block, bf16),
            pltpu.VMEM((n // 2, 2) + block, bf16),
            pltpu.VMEM((n // 2, 2, tokens // 2, columns), bf16),
            dma((2 * pairs + 2,)),
            dma((2, n, pairs)),
            dma((n, pairs)),
            dma((CHUNKS,)),
            dma((CHUNKS,)),
            dma((blocks,)),
            dma((blocks,)),
            dma((blocks,)),
            dma((blocks,)),
            dma((pieces,)),
            dma((pieces,)),
            dma((pieces,)),
            dma((pieces,)),
        ] + sums,
        compiler_params=pltpu.CompilerParams(
            collective_id=0, has_side_effects=True, vmem_limit_bytes=60 * 2**20
        ),
    )(key_rows, value_rows, queries, out_weight)


def hubs_fit(mesh, queries, out_weight):
    shape = mesh.shape
    tokens, width = queries[0] // (shape["groups"] * shape["ctx"]), queries[1] // (shape["head"] * shape["sub"])
    columns = out_weight[1] // shape["ctx"]
    sizes = (shape["groups"], shape["ctx"], shape["head"], shape["sub"]) == (2, 4, 2, 2)
    heads = width // HD
    return sizes and tokens == 3 * BLOCK and columns == 5 * TILE and heads == 2 * CHUNKS and heads * KVH == 2 * QH


def solution(mesh):
    assert mesh.shape["sub"] == 2
    assert mesh.shape["ctx"] == mesh.shape["head"] * mesh.shape["sub"]

    def run(queries, key_rows, value_rows, out_weight):
        fits = hubs_fit(mesh, queries.shape, out_weight.shape)
        return jax.shard_map(
            with_hubs if fits else on_device,
            mesh=mesh,
            in_specs=(
                P(("groups", "ctx"), ("head", "sub")),
                P(("groups", "ctx"), "head"),
                P(("groups", "ctx"), "head"),
                P(("head", "sub"), "ctx"),
            ),
            out_specs=P(("groups", "ctx"), ("head", "sub")),
            check_vma=False,
        )(queries, key_rows, value_rows, out_weight)

    return run
```

```python
import functools
import math

import jax
import jax.numpy as jnp
from jax import lax
from jax.experimental import pallas as pl
from jax.experimental.pallas import tpu as pltpu
from jax.sharding import PartitionSpec as P

QH = 64
KVH = 8
HD = 128
CHUNKS = 8
TILE = 256
ROWS = 128
MESH = pl.DeviceIdType.MESH
BLOCK = 128
EARLY = 2
SPLIT = 4
TOGETHER = 4
ORDER = ("w",) * 8 + (0, 1, 2) + ("w",) * 13


def kernel(
    n, n_head, per_pair, pairs, chunks, parts, k_hbm, v_hbm, q_hbm, w_hbm, o_ref,
    kv_all, v_ext, q_ref, att, w, own, out, rx1, summed, rx2, final,
    load_sems, kv_send, kv_recv, a_send, a_recv, s1, r1, s2, r2, s3, r3,
):
    me, head, sub = (lax.axis_index(a) for a in ("ctx", "head", "sub"))
    other = 1 - sub
    hs = head * 2 + sub
    tokens, width = q_ref.shape
    heads = width // HD
    columns = w.shape[1]
    piece = width // chunks
    to_right, to_left = me < n - 1, me > 0
    right, left = lax.min(me + 1, n - 1), lax.max(me - 1, 0)
    away = hs != me
    share = tokens // n_head

    def rows_of(b):
        return pl.ds(pl.multiple_of(b * tokens, tokens), tokens)

    first = pl.multiple_of((sub * heads // (QH // KVH)) * HD, HD)
    loads = [
        pltpu.make_async_copy(
            side.at[:, pl.ds(first, pairs * HD)],
            kv_all.at[rows_of(me), pl.ds(i * pairs * HD, pairs * HD)],
            load_sems.at[i],
        )
        for i, side in enumerate((k_hbm, v_hbm))
    ]
    loads.append(pltpu.make_async_copy(q_hbm, q_ref, load_sems.at[2]))
    loads.append(pltpu.make_async_copy(w_hbm, w, load_sems.at[3]))
    for load in loads:
        load.start()

    barrier = pltpu.get_barrier_semaphore()

    def greet(where):
        pl.semaphore_signal(barrier, inc=1, device_id=where, device_id_type=MESH)

    pl.when(to_right)(lambda: greet({"ctx": right}))
    pl.when(to_left)(lambda: greet({"ctx": left}))
    for h in range(n_head):
        source = {"ctx": hs, "head": h, "sub": me % 2}
        pl.when(jnp.logical_or(away, head != h))(functools.partial(greet, source))
    greet({"sub": other})
    for step in range(1, n_head):
        greet({"head": lax.rem(head + step, n_head)})
    count = 2 * n_head - 1 + to_right.astype(jnp.int32) + to_left.astype(jnp.int32)
    pl.semaphore_wait(barrier, count + away.astype(jnp.int32))

    def remote(src, dst, send, recv, where):
        return pltpu.make_async_remote_copy(
            src_ref=src, dst_ref=dst, send_sem=send, recv_sem=recv, device_id=where, device_id_type=MESH
        )

    def kv_copy(b, way, d):
        where = {"ctx": right if way == 0 else left}
        part = kv_all.at[rows_of(b)]
        return remote(part, part, kv_send.at[way, d], kv_recv.at[b], where)

    loads[0].wait()
    loads[1].wait()
    pl.when(to_right)(lambda: kv_copy(me, 0, 0).start())
    pl.when(to_left)(lambda: kv_copy(me, 1, 0).start())

    @pl.loop(1, n)
    def _(d):
        @pl.when(me - d >= 0)
        def _():
            copy = kv_copy(me - d, 0, d)
            copy.wait_recv()
            pl.when(to_right)(lambda: copy.start())

        @pl.when(me + d < n)
        def _():
            copy = kv_copy(me + d, 1, d)
            copy.wait_recv()
            pl.when(to_left)(lambda: copy.start())

    loads[2].wait()

    def a_copy(b, j, way, d):
        where = {"ctx": right if way == 0 else left}
        part = att.at[b, :, pl.ds(j * piece, piece)]
        return remote(part, part, a_send.at[way, d, j], a_recv.at[b, j], where)

    factor = math.log2(math.e) / HD**0.5
    for j in range(chunks):
        if j % (chunks // pairs) == 0:
            p = j // (chunks // pairs)
            v_ext[p, :, :HD] = kv_all[:, (pairs + p) * HD : (pairs + p + 1) * HD]
            v_ext[p, :, HD:] = jnp.ones((v_ext.shape[1], HD), v_ext.dtype)

        @pl.loop(j * heads // chunks, (j + 1) * heads // chunks)
        def _(h):
            pair = h // per_pair
            cols = pl.ds(pl.multiple_of(h * HD, HD), HD)
            keys = kv_all[:, pl.ds(pl.multiple_of(pair * HD, HD), HD)]
            for start in range(0, tokens, ROWS):
                rows = pl.ds(start, ROWS)
                scores = lax.dot_general(
                    q_ref[rows, cols], keys, (((1,), (1,)), ((), ())), preferred_element_type=jnp.float32
                )
                row_max = jnp.max(scores, axis=1, keepdims=True)
                weights = jnp.exp2((scores - row_max) * factor).astype(jnp.bfloat16)
                both = jnp.dot(weights, v_ext[pair], preferred_element_type=jnp.float32)
                att[me, rows, cols] = (both[:, :HD] / both[:, HD:]).astype(att.dtype)

        pl.when(to_right)(lambda: a_copy(me, j, 0, 0).start())
        pl.when(to_left)(lambda: a_copy(me, j, 1, 0).start())

    loads[3].wait()
    tile = columns // parts

    def cols_of(c):
        return pl.ds(0, columns) if parts == 1 else pl.ds(pl.multiple_of(c * tile, tile), tile)

    def core_copy(g, c):
        cols = cols_of(c)
        return remote(out.at[g, :, cols], rx1.at[g, :, cols], s1.at[g, c], r1.at[g, c], {"sub": other})

    def share_of(h):
        return pl.ds(pl.multiple_of(h * share, share), share)

    def head_copy(g, step, c):
        cols, target = cols_of(c), lax.rem(head + step, n_head)
        return remote(
            summed.at[g, share_of(target), cols], rx2.at[g, head, :, cols],
            s2.at[g, step - 1, c], r2.at[g, head, c], {"head": target},
        )

    def head_arrival(g, source, c):
        cols = cols_of(c)
        return remote(
            summed.at[g, share_of(source), cols], rx2.at[g, source, :, cols],
            s2.at[g, 0, c], r2.at[g, source, c], {"head": source},
        )

    def last_copy(g, h, c):
        cols = cols_of(c)
        where = {"ctx": 2 * g + sub, "head": me // 2, "sub": me % 2}
        return remote(final.at[g, :, cols], o_ref.at[share_of(h), cols], s3.at[g, c], r3.at[h, c], where)

    def product(t, c):
        cols = cols_of(c)
        return jnp.dot(att[t], w[:, cols], preferred_element_type=jnp.float32).astype(out.dtype)

    def multiply(t):
        g = t // 2

        @pl.when(t % 2 == sub)
        def _():
            @pl.loop(0, parts)
            def _(c):
                own[g, :, cols_of(c)] = product(t, c)

        @pl.when(t % 2 != sub)
        def _():
            @pl.loop(0, parts)
            def _(c):
                out[g, :, cols_of(c)] = product(t, c)
                core_copy(g, c).start()

    def combine(t):
        g = t // 2

        @pl.when(t % 2 == sub)
        def _():
            @pl.loop(0, parts)
            def _(c):
                cols = cols_of(c)
                core_copy(g, c).wait_recv()
                total = own[g, :, cols].astype(jnp.float32) + rx1[g, :, cols].astype(jnp.float32)
                summed[g, :, cols] = total.astype(summed.dtype)
                for step in range(1, n_head):
                    head_copy(g, step, c).start()

    def finish(t):
        g = t // 2

        @pl.when(t % 2 == sub)
        def _():
            @pl.loop(0, parts)
            def _(c):
                cols = cols_of(c)
                total = summed[g, share_of(head), cols].astype(jnp.float32)
                for step in range(1, n_head):
                    source = lax.rem(head + step, n_head)
                    head_arrival(g, source, c).wait_recv()
                    total += rx2[g, source, :, cols].astype(jnp.float32)
                final[g, :, cols] = total.astype(final.dtype)
                pl.when(jnp.logical_or(away, t != me))(lambda: last_copy(g, head, c).start())

    def finish_at(d):
        pl.when(jnp.logical_and(d >= 0, me - d >= 0))(lambda: finish(me - d))
        pl.when(jnp.logical_and(d > 0, me + d < n))(lambda: finish(me + d))

    def after(d, j, last=False):
        behind, ahead = me - d + 1, me + d - 1
        if j == 0:
            pl.when(behind >= 0)(lambda: multiply(behind))
        if j == chunks // 4:
            pl.when(jnp.logical_and(ahead < n, d > 1))(lambda: multiply(ahead))
        if j == chunks // 2:
            pl.when(behind >= 0)(lambda: combine(behind))
        if j == chunks // 2 + 1:
            pl.when(jnp.logical_and(ahead < n, d > 1))(lambda: combine(ahead))
        if j == chunks - 1 and not last:
            finish_at(d - 2)

    @pl.loop(1, n)
    def _(d):
        for j in range(chunks):

            @pl.when(me - d >= 0)
            def _():
                copy = a_copy(me - d, j, 0, d)
                copy.wait_recv()
                pl.when(to_right)(lambda: copy.start())

            @pl.when(me + d < n)
            def _():
                copy = a_copy(me + d, j, 1, d)
                copy.wait_recv()
                pl.when(to_left)(lambda: copy.start())

            after(d, j)

    finish_at(n - 2)
    for j in range(chunks):
        after(n, j, last=True)
    finish_at(n - 1)

    @pl.when(jnp.logical_not(away))
    def _():
        keep = pltpu.make_async_copy(final.at[me // 2], o_ref.at[share_of(head)], load_sems.at[0])
        keep.start()
        keep.wait()

    for h in range(n_head):

        @pl.when(jnp.logical_or(away, head != h))
        def _():
            @pl.loop(0, parts)
            def _(c):
                last_copy(0, h, c).wait_recv()

    @pl.loop(0, n)
    def _(d):
        for way, fits, go in ((0, me - d >= 0, to_right), (1, me + d < n, to_left)):
            b = me - d if way == 0 else me + d

            @pl.when(jnp.logical_and(fits, go))
            def _():
                kv_copy(b, way, d).wait_send()
                for j in range(chunks):
                    a_copy(b, j, way, d).wait_send()

    @pl.loop(0, n // 2)
    def _(g):
        @pl.loop(0, parts)
        def _(c):
            core_copy(g, c).wait_send()
            for step in range(1, n_head):
                head_copy(g, step, c).wait_send()
            pl.when(jnp.logical_or(away, 2 * g + sub != me))(lambda: last_copy(g, head, c).wait_send())


def on_device(queries, key_rows, value_rows, out_weight):
    tokens, width = queries.shape
    heads_here = width // HD
    group_ratio = QH // KVH
    pairs = max(heads_here // group_ratio, 1)
    per_pair = heads_here // pairs
    n = lax.axis_size("ctx")
    n_head = lax.axis_size("head")
    columns = out_weight.shape[1]
    block = (tokens, columns)
    groups = (n // 2,) + block
    chunks = min(CHUNKS, heads_here)
    parts = columns // TILE if columns % TILE == 0 else 1
    anywhere = pl.BlockSpec(memory_space=pl.ANY)
    dma = pltpu.SemaphoreType.DMA
    bf16 = jnp.bfloat16
    return pl.pallas_call(
        functools.partial(kernel, n, n_head, per_pair, pairs, chunks, parts),
        out_shape=jax.ShapeDtypeStruct(block, bf16),
        in_specs=[anywhere] * 4,
        out_specs=anywhere,
        scratch_shapes=[
            pltpu.VMEM((n * tokens, 2 * pairs * HD), bf16),
            pltpu.VMEM((pairs, n * tokens, 2 * HD), bf16),
            pltpu.VMEM((tokens, width), bf16),
            pltpu.VMEM((n, tokens, width), bf16),
            pltpu.VMEM(out_weight.shape, bf16),
            pltpu.VMEM(groups, bf16),
            pltpu.VMEM(groups, bf16),
            pltpu.VMEM(groups, bf16),
            pltpu.VMEM(groups, bf16),
            pltpu.VMEM((n // 2, n_head, tokens // n_head, columns), bf16),
            pltpu.VMEM((n // 2, tokens // n_head, columns), bf16),
            dma((4,)),
            dma((2, n)),
            dma((n,)),
            dma((2, n, chunks)),
            dma((n, chunks)),
            dma((n // 2, parts)),
            dma((n // 2, parts)),
            dma((n // 2, n_head - 1, parts)),
            dma((n // 2, n_head, parts)),
            dma((n // 2, parts)),
            dma((n_head, parts)),
        ],
        compiler_params=pltpu.CompilerParams(
            collective_id=0, has_side_effects=True, vmem_limit_bytes=60 * 2**20
        ),
    )(key_rows, value_rows, queries, out_weight)


def pieces_of(width, tiles):
    depth = width // (2 * SPLIT)
    cuts = [(i, k * depth, depth) for i in range(tiles) for k in range(SPLIT)]
    at, row, _ = cuts.pop()
    return cuts + [(at, row, depth // 2), (at, row + depth // 2, depth // 2)]


def hub_kernel(
    n, n_head, per_pair, pairs, chunks, tile, k_hbm, v_hbm, q_hbm, w_hbm, o_ref,
    kv_all, v_ext, q_ref, att, w, w_far, part, rx1, rx2, acc, landing,
    load_sems, kv_send, kv_recv, a_send, a_recv, e_send, e_recv, f_send, f_recv,
    w_send, w_recv, y_send, y_recv, s1, r1, s2, r2, s3, r3,
):
    me, head, sub, group = (lax.axis_index(a) for a in ("ctx", "head", "sub", "groups"))
    tokens, width = q_ref.shape
    heads = width // HD
    columns = w.shape[1]
    blocks = tokens // BLOCK
    tiles = columns // tile
    cuts = pieces_of(width, tiles)
    pieces = len(cuts)
    low = n // 2 - 1
    is_hub = jnp.logical_and(me >= low, me <= low + 1)
    is_end = jnp.logical_not(is_hub)
    to_right, to_left = me < n - 1, me > 0
    right, left = lax.min(me + 1, n - 1), lax.max(me - 1, 0)
    other = n - 1 - me
    end = jnp.where(me <= low, 0, n - 1)
    far_end = n - 1 - end
    my_hub = jnp.where(me <= low, low, low + 1)
    side = me - low
    away_head, away_sub, away_group = 1 - head, 1 - sub, 1 - group

    def rows_of(b):
        return pl.ds(pl.multiple_of(b * tokens, tokens), tokens)

    first = pl.multiple_of((sub * heads // (QH // KVH)) * HD, HD)
    loads = []
    for p in range(pairs):
        for i, ref in enumerate((k_hbm, v_hbm)):
            loads.append(pltpu.make_async_copy(
                ref.at[:, pl.ds(pl.multiple_of(first + p * HD, HD), HD)],
                kv_all.at[rows_of(me), pl.ds((2 * p + i) * HD, HD)],
                load_sems.at[2 * p + i],
            ))
    load_w = pltpu.make_async_copy(w_hbm, w, load_sems.at[2 * pairs])
    load_q = pltpu.make_async_copy(q_hbm, q_ref, load_sems.at[2 * pairs + 1])
    for load in loads + [load_w, load_q]:
        load.start()

    barrier = pltpu.get_barrier_semaphore()

    def greet(where):
        pl.semaphore_signal(barrier, inc=1, device_id=where, device_id_type=MESH)

    pl.when(to_right)(lambda: greet({"ctx": right}))
    pl.when(to_left)(lambda: greet({"ctx": left}))
    greet({"sub": away_sub})
    greet({"head": away_head})
    greet({"groups": away_group})
    origin = low + head
    mine = jnp.logical_and(me == origin, sub == me % 2)
    for h in range(n_head):
        source = {"ctx": origin, "head": h, "sub": me % 2}
        pl.when(jnp.logical_not(jnp.logical_and(mine, head == h)))(functools.partial(greet, source))
    keeps = jnp.logical_and(is_hub, jnp.logical_and(head == side, sub == me % 2))
    count = 3 + to_right.astype(jnp.int32) + to_left.astype(jnp.int32)
    count += jnp.where(is_hub, 4, 0) - keeps.astype(jnp.int32)
    pl.semaphore_wait(barrier, count)

    def remote(src, dst, send, recv, where):
        return pltpu.make_async_remote_copy(
            src_ref=src, dst_ref=dst, send_sem=send, recv_sem=recv, device_id=where, device_id_type=MESH
        )

    def kv_copy(b, way, d, p):
        where = {"ctx": right if way == 0 else left}
        block = kv_all.at[rows_of(b), pl.ds(2 * p * HD, 2 * HD)]
        return remote(block, block, kv_send.at[way, d, p], kv_recv.at[b, p], where)

    for p in range(pairs):
        loads[2 * p].wait()
        loads[2 * p + 1].wait()
        pl.when(to_right)(lambda: kv_copy(me, 0, 0, p).start())
        pl.when(to_left)(lambda: kv_copy(me, 1, 0, p).start())

    def pass_on(d, p):
        @pl.when(me - d >= 0)
        def _():
            copy = kv_copy(me - d, 0, d, p)
            copy.wait_recv()
            pl.when(to_right)(lambda: copy.start())

        @pl.when(me + d < n)
        def _():
            copy = kv_copy(me + d, 1, d, p)
            copy.wait_recv()
            pl.when(to_left)(lambda: copy.start())

    def w_piece(g, i):
        at, row, depth = cuts[i]
        rows = pl.ds(pl.multiple_of(g * (width // 2) + row, depth), depth)
        return rows, pl.ds(at * tile, tile)

    def w_copy(i):
        at = w_piece(group, i)
        return remote(w.at[at], w_far.at[at], w_send.at[i], w_recv.at[i], {"ctx": my_hub})

    def y_copy(g, i):
        at = w_piece(g, i)
        return remote(w_far.at[at], w_far.at[at], y_send.at[i], y_recv.at[i], {"groups": away_group})

    def relay_w(*which):
        for i in which:
            w_copy(i).wait_recv()
            y_copy(group, i).start()

    def await_w(*which):
        for i in which:
            y_copy(away_group, i).wait_recv()

    load_w.wait()
    ahead = ORDER.index(0)

    @pl.when(is_end)
    def _():
        for i in range(ahead):
            w_copy(i).start()

    chunk = width // chunks

    def chunk_copy(b, j):
        at = att.at[b, :, pl.ds(j * chunk, chunk)]
        return remote(at, at, a_send.at[j], a_recv.at[j], {"ctx": other})

    def end_copy(r):
        at = att.at[end, pl.ds(r * BLOCK, BLOCK)]
        return remote(at, at, e_send.at[r], e_recv.at[r], {"ctx": my_hub})

    def far_copy(b, r):
        at = att.at[b, pl.ds(r * BLOCK, BLOCK)]
        return remote(at, at, f_send.at[r], f_recv.at[r], {"ctx": other})

    for d in range(1, n):
        pass_on(d, 0)
        if d == 1:
            for p in range(1, pairs):
                pass_on(d, p)
    load_q.wait()

    factor = math.log2(math.e) / HD**0.5
    per_chunk = heads // chunks

    def prepare(p):
        v_ext[p, :, :HD] = kv_all[:, (2 * p + 1) * HD : (2 * p + 2) * HD]
        v_ext[p, :, HD:] = jnp.ones((v_ext.shape[1], HD), v_ext.dtype)

    def attend(h, p, start):
        rows, cols = pl.ds(start, ROWS), pl.ds(pl.multiple_of(h * HD, HD), HD)
        keys = kv_all[:, 2 * p * HD : (2 * p + 1) * HD]
        scores = lax.dot_general(
            q_ref[rows, cols], keys, (((1,), (1,)), ((), ())), preferred_element_type=jnp.float32
        )
        row_max = jnp.max(scores, axis=1, keepdims=True)
        weights = jnp.exp2((scores - row_max) * factor).astype(jnp.bfloat16)
        both = jnp.dot(weights, v_ext[p], preferred_element_type=jnp.float32)
        att[me, rows, cols] = (both[:, :HD] / both[:, HD:]).astype(att.dtype)

    def rest_of_pairs():
        for d in range(2, n):
            for p in range(1, pairs):
                pass_on(d, p)

    @pl.when(is_hub)
    def _():
        relay_w(0)
        for j in range(chunks):
            p = j * per_chunk // per_pair
            if (j * per_chunk) % per_pair == 0:
                prepare(p)

            @pl.loop(j * per_chunk, (j + 1) * per_chunk)
            def _(h):
                for start in range(0, tokens, ROWS):
                    attend(h, p, start)

            chunk_copy(me, j).start()
            if j == 1:
                rest_of_pairs()
            if j + 1 < chunks:
                relay_w(j + 1)

    @pl.when(is_end)
    def _():
        i = ahead
        prepare(0)
        for r in range(blocks):
            for p in range(pairs):
                if r == 0 and p == 1:
                    rest_of_pairs()
                    for q in range(1, pairs):
                        prepare(q)

                @pl.loop(p * per_pair, (p + 1) * per_pair, step=TOGETHER)
                def _(h):
                    for k in range(TOGETHER):
                        for start in range(r * BLOCK, (r + 1) * BLOCK, ROWS):
                            attend(h + k, p, start)

            end_copy(r).start()
            after = ORDER.index(r) + 1
            while after < len(ORDER) and ORDER[after] == "w":
                w_copy(i).start()
                i, after = i + 1, after + 1

    late = tiles - EARLY

    def geometry(kind, r):
        if kind == "near":
            return 0, r * BLOCK, BLOCK, 0, tiles, r
        if kind == "early":
            return 1, r * BLOCK, BLOCK, 0, EARLY, blocks + r
        return 1, 0, tokens, r, 1, 2 * blocks + r - EARLY

    def region(kind, r, half=None):
        cb, row, m, c, k, index = geometry(kind, r)
        if half is not None:
            row, m = row + half * (m // 2), m // 2
            row = row if isinstance(row, int) else pl.multiple_of(row, m)
        return cb, pl.ds(row, m), pl.ds(c * tile, k * tile), index

    def product(t, row, m, cb, c, k):
        source = w_far if cb else w

        @pl.loop(c, c + k)
        def _(i):
            cols = pl.ds(pl.multiple_of(i * tile, tile), tile)
            part[t, cb, pl.ds(row, m), cols] = jnp.dot(
                att[t, pl.ds(row, m)], source[:, cols], preferred_element_type=jnp.float32
            ).astype(part.dtype)

    def core_copy(t, kind, r):
        cb, rows, cols, index = region(kind, r)
        return remote(
            part.at[t, cb, rows, cols], rx1.at[t // 2, cb, rows, cols],
            s1.at[t // 2, index], r1.at[t // 2, index], {"sub": away_sub},
        )

    def head_copy(t, kind, r):
        cb, rows, cols, index = region(kind, r, away_head)
        half, short = geometry(kind, r)[1] // 2, geometry(kind, r)[2] // 2
        return remote(
            part.at[t, cb, rows, cols], rx2.at[t // 2, cb, pl.ds(half, short), cols],
            s2.at[t // 2, index], r2.at[t // 2, index], {"head": away_head},
        )

    def is_kept(t, cb):
        if cb:
            return jnp.bool_(False)
        return jnp.logical_and(t == me, keeps)

    def last_copy(t, kind, r):
        cb, rows, cols, index = region(kind, r, head)
        where = {"ctx": t, "head": side, "sub": (me + cb) % 2}
        return remote(
            part.at[t, cb, rows, cols], o_ref.at[rows, cols], s3.at[t // 2, index], r3.at[head, index], where
        )

    def whole_copy(t, kind, r):
        cb, rows, cols, index = region(kind, r)
        where = {"ctx": t, "head": side, "sub": (me + cb) % 2}
        return remote(
            part.at[t, cb, rows, cols], landing.at[head], s3.at[t // 2, index], r3.at[head, index], where
        )

    def is_last(kind, r):
        return kind == "late" and r == tiles - 1

    def keep_copy(t, kind, r):
        cb, rows, cols, index = region(kind, r, head)
        return pltpu.make_async_copy(part.at[t, cb, rows, cols], o_ref.at[rows, cols], s3.at[t // 2, index])

    def owns(t):
        return t % 2 == sub

    def send(jobs):
        for t, kind, r in jobs:
            pl.when(jnp.logical_not(owns(t)))(functools.partial(lambda *a: core_copy(*a).start(), t, kind, r))

    def multiply(*jobs):
        for t, kind, r in jobs:
            cb, row, m, c, k, _ = geometry(kind, r)
            product(t, row, m, cb, c, k)
            send([(t, kind, r)])

    def slab(t, k):
        last = pl.ds((tiles - 1) * tile, tile)
        total = None
        for g in range(2):
            depth = pl.ds(g * (width // 2) + k * (width // 2 // SPLIT), width // 2 // SPLIT)
            term = jnp.dot(att[t, :, depth], w_far[depth, last], preferred_element_type=jnp.float32)
            total = term if total is None else total + term
        return total

    def begin(*toks):
        for t in toks:
            acc[t] = slab(t, 0) + slab(t, 1)

    def extend(*toks):
        for t in toks:
            acc[t] += slab(t, 2)

    def complete(*jobs):
        for t, kind, r in jobs:
            total = acc[t] + slab(t, 3)
            part[t, 1, :, pl.ds((tiles - 1) * tile, tile)] = total.astype(part.dtype)
            send([(t, kind, r)])

    def multiply_all(t, kind):
        cb, _, _, c, k, _ = geometry(kind, 0)
        product(t, 0, tokens, cb, c, k)
        send([(t, kind, r) for r in range(blocks)])

    def combine(*jobs):
        for t, kind, r in jobs:

            @pl.when(owns(t))
            def _():
                cb, rows, cols, _ = region(kind, r)
                core_copy(t, kind, r).wait_recv()
                total = part[t, cb, rows, cols].astype(jnp.float32)
                total += rx1[t // 2, cb, rows, cols].astype(jnp.float32)
                part[t, cb, rows, cols] = total.astype(part.dtype)
                (whole_copy if is_last(kind, r) else head_copy)(t, kind, r).start()

    def finish(*jobs):
        for t, kind, r in jobs:

            @pl.when(owns(t))
            def _():
                cb, rows, cols, _ = region(kind, r, head)
                half, short = geometry(kind, r)[1] // 2, geometry(kind, r)[2] // 2
                head_copy(t, kind, r).wait_recv()
                total = part[t, cb, rows, cols].astype(jnp.float32)
                total += rx2[t // 2, cb, pl.ds(half, short), cols].astype(jnp.float32)
                part[t, cb, rows, cols] = total.astype(part.dtype)
                if cb:
                    last_copy(t, kind, r).start()
                else:
                    pl.when(is_kept(t, cb))(lambda: keep_copy(t, kind, r).start())
                    pl.when(jnp.logical_not(is_kept(t, cb)))(lambda: last_copy(t, kind, r).start())

    def relay_end(r):
        end_copy(r).wait_recv()
        far_copy(end, r).start()

    def await_far(r):
        far_copy(far_end, r).wait_recv()

    def all_rows(t, kind):
        return [(t, kind, r) for r in range(blocks)]

    def both(t, r):
        return [(t, "near", r), (t, "early", r)]

    @pl.when(is_hub)
    def _():
        g0, g1 = all_rows(me, "near"), all_rows(me, "early")
        g2, g5, g9 = both(end, 0), both(end, 1), both(end, 2)
        g3, g4 = all_rows(other, "near"), all_rows(other, "early")
        g6, g7, g11 = both(far_end, 0), both(far_end, 1), both(far_end, 2)

        def late_of(i, *toks):
            return [(t, "late", i) for t in toks]

        g8, g10 = late_of(2, me, other, end), late_of(3, far_end, other, end, me)
        g11 = g11 + late_of(2, far_end)
        g12, g13 = late_of(4, far_end, other), late_of(4, end, me)

        multiply_all(me, "near")
        await_w(*range(8))
        multiply_all(me, "early")
        combine(*g0)
        combine(*g1)
        relay_end(0)
        multiply(*g2)
        combine(*g2)
        finish(*g0)
        finish(*g1)
        for j in range(chunks):
            chunk_copy(other, j).wait_recv()
        multiply_all(other, "near")
        relay_end(1)
        multiply_all(other, "early")
        combine(*g3)
        combine(*g4)
        multiply(*g5)
        finish(*g2)
        combine(*g5)
        await_far(0)
        multiply(*g6)
        relay_end(2)
        combine(*g6)
        multiply(*g9)
        relay_w(8)
        combine(*g9)
        finish(*g3)
        relay_w(9)
        finish(*g4)
        relay_w(10)
        finish(*g5)
        await_far(1)
        multiply(*g7)
        relay_w(11)
        combine(*g7)
        finish(*g6)
        relay_w(12)
        await_w(8, 9, 10, 11)
        multiply(*g8)
        relay_w(13)
        combine(*g8)
        finish(*g9)
        await_far(2)
        relay_w(14)
        multiply(*g11[:2])
        relay_w(15)
        multiply(*g11[2:])
        combine(*g11)
        finish(*g7)
        relay_w(16)
        relay_w(17)
        await_w(12, 13, 14, 15)
        multiply(*g10[:2])
        relay_w(18)
        multiply(*g10[2:])
        relay_w(19)
        combine(*g10)
        relay_w(20)
        finish(*g8)
        finish(*g11)
        await_w(16, 17)
        begin(far_end, other, end, me)
        await_w(18)
        extend(far_end, other, end, me)
        finish(*g10)
        await_w(19, 20)
        complete(*g12)
        complete(*g13)
        combine(*g12)
        combine(*g13)

    for way, go in ((0, to_right), (1, to_left)):
        for d in range(n):
            b = me - d if way == 0 else me + d
            fits = b >= 0 if way == 0 else b < n

            @pl.when(jnp.logical_and(fits, go))
            def _():
                for p in range(pairs):
                    kv_copy(b, way, d, p).wait_send()

    @pl.when(is_end)
    def _():
        for i in range(pieces):
            w_copy(i).wait_send()
        for r in range(blocks):
            end_copy(r).wait_send()

    @pl.when(is_hub)
    def _():
        for i in range(pieces):
            y_copy(group, i).wait_send()
        for j in range(chunks):
            chunk_copy(me, j).wait_send()
        for r in range(blocks):
            far_copy(end, r).wait_send()
        names = [("near", r) for r in range(blocks)] + [("early", r) for r in range(blocks)]
        names += [("late", r) for r in range(EARLY, tiles)]
        for t in (me, other, end, far_end):
            for kind, r in names:

                @pl.when(owns(t))
                def _():
                    if is_last(kind, r):
                        whole_copy(t, kind, r).wait_send()
                        return
                    head_copy(t, kind, r).wait_send()
                    if kind == "near":
                        kept = is_kept(t, 0)
                        pl.when(kept)(lambda: keep_copy(t, kind, r).wait())
                        pl.when(jnp.logical_not(kept))(lambda: last_copy(t, kind, r).wait_send())
                    else:
                        last_copy(t, kind, r).wait_send()

                @pl.when(jnp.logical_not(owns(t)))
                def _():
                    core_copy(t, kind, r).wait_send()

    my_cb = (sub + 1 + head) % 2

    def arrivals(cb):
        kinds = [("near", r) for r in range(blocks)]
        if cb:
            kinds = [("early", r) for r in range(blocks)] + [("late", r) for r in range(EARLY, tiles - 1)]
        for kind, r in kinds:
            for h in range(n_head):
                cb_, rows, cols, index = region(kind, r, h)
                got = remote(
                    part.at[0, cb_, rows, cols], o_ref.at[rows, cols], s3.at[0, index], r3.at[h, index],
                    {"ctx": origin, "head": h, "sub": me % 2},
                )
                if cb:
                    got.wait_recv()
                else:
                    pl.when(jnp.logical_not(jnp.logical_and(mine, head == h)))(lambda: got.wait_recv())
        if cb:
            cb_, rows, cols, index = region("late", tiles - 1)
            for h in range(n_head):
                remote(
                    part.at[0, cb_, rows, cols], landing.at[h], s3.at[0, index], r3.at[h, index],
                    {"ctx": origin, "head": h, "sub": me % 2},
                ).wait_recv()
            total = landing[0].astype(jnp.float32)
            for h in range(1, n_head):
                total += landing[h].astype(jnp.float32)
            landing[0] = total.astype(landing.dtype)
            place = pltpu.make_async_copy(landing.at[0], o_ref.at[rows, cols], load_sems.at[0])
            place.start()
            place.wait()

    pl.when(my_cb == 0)(lambda: arrivals(0))
    pl.when(my_cb == 1)(lambda: arrivals(1))


def with_hubs(queries, key_rows, value_rows, out_weight):
    tokens, width = queries.shape
    heads_here = width // HD
    pairs = heads_here // (QH // KVH)
    per_pair = heads_here // pairs
    n = lax.axis_size("ctx")
    n_head = lax.axis_size("head")
    columns = out_weight.shape[1]
    block = (tokens, columns)
    tiles = columns // TILE
    pieces = len(pieces_of(width, tiles))
    blocks = tokens // BLOCK
    kinds = 2 * blocks + tiles - EARLY
    anywhere = pl.BlockSpec(memory_space=pl.ANY)
    dma = pltpu.SemaphoreType.DMA
    bf16 = jnp.bfloat16
    sums = [dma((n // 2, kinds))] * 5 + [dma((n_head, kinds))]
    return pl.pallas_call(
        functools.partial(hub_kernel, n, n_head, per_pair, pairs, CHUNKS, TILE),
        out_shape=jax.ShapeDtypeStruct(block, bf16),
        in_specs=[anywhere] * 4,
        out_specs=anywhere,
        scratch_shapes=[
            pltpu.VMEM((n * tokens, 2 * pairs * HD), bf16),
            pltpu.VMEM((pairs, n * tokens, 2 * HD), bf16),
            pltpu.VMEM((tokens, width), bf16),
            pltpu.VMEM((n, tokens, width), bf16),
            pltpu.VMEM(out_weight.shape, bf16),
            pltpu.VMEM(out_weight.shape, bf16),
            pltpu.VMEM((n, 2) + block, bf16),
            pltpu.VMEM((n // 2, 2) + block, bf16),
            pltpu.VMEM((n // 2, 2, tokens // 2, columns), bf16),
            pltpu.VMEM((n, tokens, TILE), jnp.float32),
            pltpu.VMEM((n_head, tokens, TILE), bf16),
            dma((2 * pairs + 2,)),
            dma((2, n, pairs)),
            dma((n, pairs)),
            dma((CHUNKS,)),
            dma((CHUNKS,)),
            dma((blocks,)),
            dma((blocks,)),
            dma((blocks,)),
            dma((blocks,)),
            dma((pieces,)),
            dma((pieces,)),
            dma((pieces,)),
            dma((pieces,)),
        ] + sums,
        compiler_params=pltpu.CompilerParams(
            collective_id=0, has_side_effects=True, vmem_limit_bytes=60 * 2**20
        ),
    )(key_rows, value_rows, queries, out_weight)


def hubs_fit(mesh, queries, out_weight):
    shape = mesh.shape
    tokens, width = queries[0] // (shape["groups"] * shape["ctx"]), queries[1] // (shape["head"] * shape["sub"])
    columns = out_weight[1] // shape["ctx"]
    sizes = (shape["groups"], shape["ctx"], shape["head"], shape["sub"]) == (2, 4, 2, 2)
    heads = width // HD
    return sizes and tokens == 3 * BLOCK and columns == 5 * TILE and heads == 2 * CHUNKS and heads * KVH == 2 * QH


def solution(mesh):
    assert mesh.shape["sub"] == 2
    assert mesh.shape["ctx"] == mesh.shape["head"] * mesh.shape["sub"]

    def run(queries, key_rows, value_rows, out_weight):
        fits = hubs_fit(mesh, queries.shape, out_weight.shape)
        return jax.shard_map(
            with_hubs if fits else on_device,
            mesh=mesh,
            in_specs=(
                P(("groups", "ctx"), ("head", "sub")),
                P(("groups", "ctx"), "head"),
                P(("groups", "ctx"), "head"),
                P(("head", "sub"), "ctx"),
            ),
            out_specs=P(("groups", "ctx"), ("head", "sub")),
            check_vma=False,
        )(queries, key_rows, value_rows, out_weight)

    return run
```

```python
import functools
import math

import jax
import jax.numpy as jnp
from jax import lax
from jax.experimental import pallas as pl
from jax.experimental.pallas import tpu as pltpu
from jax.sharding import PartitionSpec as P

QH = 64
KVH = 8
HD = 128
CHUNKS = 8
TILE = 256
ROWS = 128
MESH = pl.DeviceIdType.MESH
BLOCK = 128
EARLY = 2
SPLIT = 4
TOGETHER = 4
ORDER = ("w",) * 8 + (0, 1, 2) + ("w",) * 13


def kernel(
    n, n_head, per_pair, pairs, chunks, parts, k_hbm, v_hbm, q_hbm, w_hbm, o_ref,
    kv_all, v_ext, q_ref, att, w, own, out, rx1, summed, rx2, final,
    load_sems, kv_send, kv_recv, a_send, a_recv, s1, r1, s2, r2, s3, r3,
):
    me, head, sub = (lax.axis_index(a) for a in ("ctx", "head", "sub"))
    other = 1 - sub
    hs = head * 2 + sub
    tokens, width = q_ref.shape
    heads = width // HD
    columns = w.shape[1]
    piece = width // chunks
    to_right, to_left = me < n - 1, me > 0
    right, left = lax.min(me + 1, n - 1), lax.max(me - 1, 0)
    away = hs != me
    share = tokens // n_head

    def rows_of(b):
        return pl.ds(pl.multiple_of(b * tokens, tokens), tokens)

    first = pl.multiple_of((sub * heads // (QH // KVH)) * HD, HD)
    loads = [
        pltpu.make_async_copy(
            side.at[:, pl.ds(first, pairs * HD)],
            kv_all.at[rows_of(me), pl.ds(i * pairs * HD, pairs * HD)],
            load_sems.at[i],
        )
        for i, side in enumerate((k_hbm, v_hbm))
    ]
    loads.append(pltpu.make_async_copy(q_hbm, q_ref, load_sems.at[2]))
    loads.append(pltpu.make_async_copy(w_hbm, w, load_sems.at[3]))
    for load in loads:
        load.start()

    barrier = pltpu.get_barrier_semaphore()

    def greet(where):
        pl.semaphore_signal(barrier, inc=1, device_id=where, device_id_type=MESH)

    pl.when(to_right)(lambda: greet({"ctx": right}))
    pl.when(to_left)(lambda: greet({"ctx": left}))
    for h in range(n_head):
        source = {"ctx": hs, "head": h, "sub": me % 2}
        pl.when(jnp.logical_or(away, head != h))(functools.partial(greet, source))
    greet({"sub": other})
    for step in range(1, n_head):
        greet({"head": lax.rem(head + step, n_head)})
    count = 2 * n_head - 1 + to_right.astype(jnp.int32) + to_left.astype(jnp.int32)
    pl.semaphore_wait(barrier, count + away.astype(jnp.int32))

    def remote(src, dst, send, recv, where):
        return pltpu.make_async_remote_copy(
            src_ref=src, dst_ref=dst, send_sem=send, recv_sem=recv, device_id=where, device_id_type=MESH
        )

    def kv_copy(b, way, d):
        where = {"ctx": right if way == 0 else left}
        part = kv_all.at[rows_of(b)]
        return remote(part, part, kv_send.at[way, d], kv_recv.at[b], where)

    loads[0].wait()
    loads[1].wait()
    pl.when(to_right)(lambda: kv_copy(me, 0, 0).start())
    pl.when(to_left)(lambda: kv_copy(me, 1, 0).start())

    @pl.loop(1, n)
    def _(d):
        @pl.when(me - d >= 0)
        def _():
            copy = kv_copy(me - d, 0, d)
            copy.wait_recv()
            pl.when(to_right)(lambda: copy.start())

        @pl.when(me + d < n)
        def _():
            copy = kv_copy(me + d, 1, d)
            copy.wait_recv()
            pl.when(to_left)(lambda: copy.start())

    loads[2].wait()

    def a_copy(b, j, way, d):
        where = {"ctx": right if way == 0 else left}
        part = att.at[b, :, pl.ds(j * piece, piece)]
        return remote(part, part, a_send.at[way, d, j], a_recv.at[b, j], where)

    factor = math.log2(math.e) / HD**0.5
    for j in range(chunks):
        if j % (chunks // pairs) == 0:
            p = j // (chunks // pairs)
            v_ext[p, :, :HD] = kv_all[:, (pairs + p) * HD : (pairs + p + 1) * HD]
            v_ext[p, :, HD:] = jnp.ones((v_ext.shape[1], HD), v_ext.dtype)

        @pl.loop(j * heads // chunks, (j + 1) * heads // chunks)
        def _(h):
            pair = h // per_pair
            cols = pl.ds(pl.multiple_of(h * HD, HD), HD)
            keys = kv_all[:, pl.ds(pl.multiple_of(pair * HD, HD), HD)]
            for start in range(0, tokens, ROWS):
                rows = pl.ds(start, ROWS)
                scores = lax.dot_general(
                    q_ref[rows, cols], keys, (((1,), (1,)), ((), ())), preferred_element_type=jnp.float32
                )
                row_max = jnp.max(scores, axis=1, keepdims=True)
                weights = jnp.exp2((scores - row_max) * factor).astype(jnp.bfloat16)
                both = jnp.dot(weights, v_ext[pair], preferred_element_type=jnp.float32)
                att[me, rows, cols] = (both[:, :HD] / both[:, HD:]).astype(att.dtype)

        pl.when(to_right)(lambda: a_copy(me, j, 0, 0).start())
        pl.when(to_left)(lambda: a_copy(me, j, 1, 0).start())

    loads[3].wait()
    tile = columns // parts

    def cols_of(c):
        return pl.ds(0, columns) if parts == 1 else pl.ds(pl.multiple_of(c * tile, tile), tile)

    def core_copy(g, c):
        cols = cols_of(c)
        return remote(out.at[g, :, cols], rx1.at[g, :, cols], s1.at[g, c], r1.at[g, c], {"sub": other})

    def share_of(h):
        return pl.ds(pl.multiple_of(h * share, share), share)

    def head_copy(g, step, c):
        cols, target = cols_of(c), lax.rem(head + step, n_head)
        return remote(
            summed.at[g, share_of(target), cols], rx2.at[g, head, :, cols],
            s2.at[g, step - 1, c], r2.at[g, head, c], {"head": target},
        )

    def head_arrival(g, source, c):
        cols = cols_of(c)
        return remote(
            summed.at[g, share_of(source), cols], rx2.at[g, source, :, cols],
            s2.at[g, 0, c], r2.at[g, source, c], {"head": source},
        )

    def last_copy(g, h, c):
        cols = cols_of(c)
        where = {"ctx": 2 * g + sub, "head": me // 2, "sub": me % 2}
        return remote(final.at[g, :, cols], o_ref.at[share_of(h), cols], s3.at[g, c], r3.at[h, c], where)

    def product(t, c):
        cols = cols_of(c)
        return jnp.dot(att[t], w[:, cols], preferred_element_type=jnp.float32).astype(out.dtype)

    def multiply(t):
        g = t // 2

        @pl.when(t % 2 == sub)
        def _():
            @pl.loop(0, parts)
            def _(c):
                own[g, :, cols_of(c)] = product(t, c)

        @pl.when(t % 2 != sub)
        def _():
            @pl.loop(0, parts)
            def _(c):
                out[g, :, cols_of(c)] = product(t, c)
                core_copy(g, c).start()

    def combine(t):
        g = t // 2

        @pl.when(t % 2 == sub)
        def _():
            @pl.loop(0, parts)
            def _(c):
                cols = cols_of(c)
                core_copy(g, c).wait_recv()
                total = own[g, :, cols].astype(jnp.float32) + rx1[g, :, cols].astype(jnp.float32)
                summed[g, :, cols] = total.astype(summed.dtype)
                for step in range(1, n_head):
                    head_copy(g, step, c).start()

    def finish(t):
        g = t // 2

        @pl.when(t % 2 == sub)
        def _():
            @pl.loop(0, parts)
            def _(c):
                cols = cols_of(c)
                total = summed[g, share_of(head), cols].astype(jnp.float32)
                for step in range(1, n_head):
                    source = lax.rem(head + step, n_head)
                    head_arrival(g, source, c).wait_recv()
                    total += rx2[g, source, :, cols].astype(jnp.float32)
                final[g, :, cols] = total.astype(final.dtype)
                pl.when(jnp.logical_or(away, t != me))(lambda: last_copy(g, head, c).start())

    def finish_at(d):
        pl.when(jnp.logical_and(d >= 0, me - d >= 0))(lambda: finish(me - d))
        pl.when(jnp.logical_and(d > 0, me + d < n))(lambda: finish(me + d))

    def after(d, j, last=False):
        behind, ahead = me - d + 1, me + d - 1
        if j == 0:
            pl.when(behind >= 0)(lambda: multiply(behind))
        if j == chunks // 4:
            pl.when(jnp.logical_and(ahead < n, d > 1))(lambda: multiply(ahead))
        if j == chunks // 2:
            pl.when(behind >= 0)(lambda: combine(behind))
        if j == chunks // 2 + 1:
            pl.when(jnp.logical_and(ahead < n, d > 1))(lambda: combine(ahead))
        if j == chunks - 1 and not last:
            finish_at(d - 2)

    @pl.loop(1, n)
    def _(d):
        for j in range(chunks):

            @pl.when(me - d >= 0)
            def _():
                copy = a_copy(me - d, j, 0, d)
                copy.wait_recv()
                pl.when(to_right)(lambda: copy.start())

            @pl.when(me + d < n)
            def _():
                copy = a_copy(me + d, j, 1, d)
                copy.wait_recv()
                pl.when(to_left)(lambda: copy.start())

            after(d, j)

    finish_at(n - 2)
    for j in range(chunks):
        after(n, j, last=True)
    finish_at(n - 1)

    @pl.when(jnp.logical_not(away))
    def _():
        keep = pltpu.make_async_copy(final.at[me // 2], o_ref.at[share_of(head)], load_sems.at[0])
        keep.start()
        keep.wait()

    for h in range(n_head):

        @pl.when(jnp.logical_or(away, head != h))
        def _():
            @pl.loop(0, parts)
            def _(c):
                last_copy(0, h, c).wait_recv()

    @pl.loop(0, n)
    def _(d):
        for way, fits, go in ((0, me - d >= 0, to_right), (1, me + d < n, to_left)):
            b = me - d if way == 0 else me + d

            @pl.when(jnp.logical_and(fits, go))
            def _():
                kv_copy(b, way, d).wait_send()
                for j in range(chunks):
                    a_copy(b, j, way, d).wait_send()

    @pl.loop(0, n // 2)
    def _(g):
        @pl.loop(0, parts)
        def _(c):
            core_copy(g, c).wait_send()
            for step in range(1, n_head):
                head_copy(g, step, c).wait_send()
            pl.when(jnp.logical_or(away, 2 * g + sub != me))(lambda: last_copy(g, head, c).wait_send())


def on_device(queries, key_rows, value_rows, out_weight):
    tokens, width = queries.shape
    heads_here = width // HD
    group_ratio = QH // KVH
    pairs = max(heads_here // group_ratio, 1)
    per_pair = heads_here // pairs
    n = lax.axis_size("ctx")
    n_head = lax.axis_size("head")
    columns = out_weight.shape[1]
    block = (tokens, columns)
    groups = (n // 2,) + block
    chunks = min(CHUNKS, heads_here)
    parts = columns // TILE if columns % TILE == 0 else 1
    anywhere = pl.BlockSpec(memory_space=pl.ANY)
    dma = pltpu.SemaphoreType.DMA
    bf16 = jnp.bfloat16
    return pl.pallas_call(
        functools.partial(kernel, n, n_head, per_pair, pairs, chunks, parts),
        out_shape=jax.ShapeDtypeStruct(block, bf16),
        in_specs=[anywhere] * 4,
        out_specs=anywhere,
        scratch_shapes=[
            pltpu.VMEM((n * tokens, 2 * pairs * HD), bf16),
            pltpu.VMEM((pairs, n * tokens, 2 * HD), bf16),
            pltpu.VMEM((tokens, width), bf16),
            pltpu.VMEM((n, tokens, width), bf16),
            pltpu.VMEM(out_weight.shape, bf16),
            pltpu.VMEM(groups, bf16),
            pltpu.VMEM(groups, bf16),
            pltpu.VMEM(groups, bf16),
            pltpu.VMEM(groups, bf16),
            pltpu.VMEM((n // 2, n_head, tokens // n_head, columns), bf16),
            pltpu.VMEM((n // 2, tokens // n_head, columns), bf16),
            dma((4,)),
            dma((2, n)),
            dma((n,)),
            dma((2, n, chunks)),
            dma((n, chunks)),
            dma((n // 2, parts)),
            dma((n // 2, parts)),
            dma((n // 2, n_head - 1, parts)),
            dma((n // 2, n_head, parts)),
            dma((n // 2, parts)),
            dma((n_head, parts)),
        ],
        compiler_params=pltpu.CompilerParams(
            collective_id=0, has_side_effects=True, vmem_limit_bytes=60 * 2**20
        ),
    )(key_rows, value_rows, queries, out_weight)


def pieces_of(width, tiles):
    depth = width // (2 * SPLIT)
    cuts = [(i, k * depth, depth) for i in range(tiles) for k in range(SPLIT)]
    at, row, _ = cuts.pop()
    return cuts + [(at, row, depth // 2), (at, row + depth // 2, depth // 2)]


def hub_kernel(
    n, n_head, per_pair, pairs, chunks, tile, k_hbm, v_hbm, q_hbm, w_hbm, o_ref,
    kv_all, v_ext, q_ref, att, w, w_far, part, rx1, rx2, acc, landing,
    load_sems, kv_send, kv_recv, a_send, a_recv, e_send, e_recv, f_send, f_recv,
    w_send, w_recv, y_send, y_recv, s1, r1, s2, r2, s3, r3,
):
    me, head, sub, group = (lax.axis_index(a) for a in ("ctx", "head", "sub", "groups"))
    tokens, width = q_ref.shape
    heads = width // HD
    columns = w.shape[1]
    blocks = tokens // BLOCK
    tiles = columns // tile
    cuts = pieces_of(width, tiles)
    pieces = len(cuts)
    low = n // 2 - 1
    is_hub = jnp.logical_and(me >= low, me <= low + 1)
    is_end = jnp.logical_not(is_hub)
    to_right, to_left = me < n - 1, me > 0
    right, left = lax.min(me + 1, n - 1), lax.max(me - 1, 0)
    other = n - 1 - me
    end = jnp.where(me <= low, 0, n - 1)
    far_end = n - 1 - end
    my_hub = jnp.where(me <= low, low, low + 1)
    side = me - low
    away_head, away_sub, away_group = 1 - head, 1 - sub, 1 - group

    def rows_of(b):
        return pl.ds(pl.multiple_of(b * tokens, tokens), tokens)

    first = pl.multiple_of((sub * heads // (QH // KVH)) * HD, HD)
    loads = []
    for p in range(pairs):
        for i, ref in enumerate((k_hbm, v_hbm)):
            loads.append(pltpu.make_async_copy(
                ref.at[:, pl.ds(pl.multiple_of(first + p * HD, HD), HD)],
                kv_all.at[rows_of(me), pl.ds((2 * p + i) * HD, HD)],
                load_sems.at[2 * p + i],
            ))
    load_w = pltpu.make_async_copy(w_hbm, w, load_sems.at[2 * pairs])
    load_q = pltpu.make_async_copy(q_hbm, q_ref, load_sems.at[2 * pairs + 1])
    for load in loads + [load_w, load_q]:
        load.start()

    barrier = pltpu.get_barrier_semaphore()

    def greet(where):
        pl.semaphore_signal(barrier, inc=1, device_id=where, device_id_type=MESH)

    pl.when(to_right)(lambda: greet({"ctx": right}))
    pl.when(to_left)(lambda: greet({"ctx": left}))
    greet({"sub": away_sub})
    greet({"head": away_head})
    greet({"groups": away_group})
    origin = low + head
    mine = jnp.logical_and(me == origin, sub == me % 2)
    for h in range(n_head):
        source = {"ctx": origin, "head": h, "sub": me % 2}
        pl.when(jnp.logical_not(jnp.logical_and(mine, head == h)))(functools.partial(greet, source))
    keeps = jnp.logical_and(is_hub, jnp.logical_and(head == side, sub == me % 2))
    count = 3 + to_right.astype(jnp.int32) + to_left.astype(jnp.int32)
    count += jnp.where(is_hub, 4, 0) - keeps.astype(jnp.int32)
    pl.semaphore_wait(barrier, count)

    def remote(src, dst, send, recv, where):
        return pltpu.make_async_remote_copy(
            src_ref=src, dst_ref=dst, send_sem=send, recv_sem=recv, device_id=where, device_id_type=MESH
        )

    def kv_copy(b, way, d, p):
        where = {"ctx": right if way == 0 else left}
        block = kv_all.at[rows_of(b), pl.ds(2 * p * HD, 2 * HD)]
        return remote(block, block, kv_send.at[way, d, p], kv_recv.at[b, p], where)

    for p in range(pairs):
        loads[2 * p].wait()
        loads[2 * p + 1].wait()
        pl.when(to_right)(lambda: kv_copy(me, 0, 0, p).start())
        pl.when(to_left)(lambda: kv_copy(me, 1, 0, p).start())

    def pass_on(d, p):
        @pl.when(me - d >= 0)
        def _():
            copy = kv_copy(me - d, 0, d, p)
            copy.wait_recv()
            pl.when(to_right)(lambda: copy.start())

        @pl.when(me + d < n)
        def _():
            copy = kv_copy(me + d, 1, d, p)
            copy.wait_recv()
            pl.when(to_left)(lambda: copy.start())

    def w_piece(g, i):
        at, row, depth = cuts[i]
        rows = pl.ds(pl.multiple_of(g * (width // 2) + row, depth), depth)
        return rows, pl.ds(at * tile, tile)

    def w_copy(i):
        at = w_piece(group, i)
        return remote(w.at[at], w_far.at[at], w_send.at[i], w_recv.at[i], {"ctx": my_hub})

    def y_copy(g, i):
        at = w_piece(g, i)
        return remote(w_far.at[at], w_far.at[at], y_send.at[i], y_recv.at[i], {"groups": away_group})

    def relay_w(*which):
        for i in which:
            w_copy(i).wait_recv()
            y_copy(group, i).start()

    def await_w(*which):
        for i in which:
            y_copy(away_group, i).wait_recv()

    load_w.wait()
    ahead = ORDER.index(0)

    @pl.when(is_end)
    def _():
        for i in range(ahead):
            w_copy(i).start()

    chunk = width // chunks

    def chunk_copy(b, j):
        at = att.at[b, :, pl.ds(j * chunk, chunk)]
        return remote(at, at, a_send.at[j], a_recv.at[j], {"ctx": other})

    def end_copy(r):
        at = att.at[end, pl.ds(r * BLOCK, BLOCK)]
        return remote(at, at, e_send.at[r], e_recv.at[r], {"ctx": my_hub})

    def far_copy(b, r):
        at = att.at[b, pl.ds(r * BLOCK, BLOCK)]
        return remote(at, at, f_send.at[r], f_recv.at[r], {"ctx": other})

    for d in range(1, n):
        pass_on(d, 0)
        if d == 1:
            for p in range(1, pairs):
                pass_on(d, p)
    load_q.wait()

    factor = math.log2(math.e) / HD**0.5
    per_chunk = heads // chunks

    def prepare(p):
        v_ext[p, :, :HD] = kv_all[:, (2 * p + 1) * HD : (2 * p + 2) * HD]
        v_ext[p, :, HD:] = jnp.ones((v_ext.shape[1], HD), v_ext.dtype)

    def attend(h, p, start):
        rows, cols = pl.ds(start, ROWS), pl.ds(pl.multiple_of(h * HD, HD), HD)
        keys = kv_all[:, 2 * p * HD : (2 * p + 1) * HD]
        scores = lax.dot_general(
            q_ref[rows, cols], keys, (((1,), (1,)), ((), ())), preferred_element_type=jnp.float32
        )
        row_max = jnp.max(scores, axis=1, keepdims=True)
        weights = jnp.exp2((scores - row_max) * factor).astype(jnp.bfloat16)
        both = jnp.dot(weights, v_ext[p], preferred_element_type=jnp.float32)
        att[me, rows, cols] = (both[:, :HD] / both[:, HD:]).astype(att.dtype)

    def rest_of_pairs():
        for d in range(2, n):
            for p in range(1, pairs):
                pass_on(d, p)

    @pl.when(is_hub)
    def _():
        relay_w(0)
        for j in range(chunks):
            p = j * per_chunk // per_pair
            if (j * per_chunk) % per_pair == 0:
                prepare(p)

            @pl.loop(j * per_chunk, (j + 1) * per_chunk)
            def _(h):
                for start in range(0, tokens, ROWS):
                    attend(h, p, start)

            chunk_copy(me, j).start()
            if j == 1:
                rest_of_pairs()
            if j + 1 < chunks:
                relay_w(j + 1)

    @pl.when(is_end)
    def _():
        i = ahead
        prepare(0)
        for r in range(blocks):
            for p in range(pairs):
                if r == 0 and p == 1:
                    rest_of_pairs()
                    for q in range(1, pairs):
                        prepare(q)

                @pl.loop(p * per_pair, (p + 1) * per_pair, step=TOGETHER)
                def _(h):
                    for k in range(TOGETHER):
                        for start in range(r * BLOCK, (r + 1) * BLOCK, ROWS):
                            attend(h + k, p, start)

            end_copy(r).start()
            after = ORDER.index(r) + 1
            while after < len(ORDER) and ORDER[after] == "w":
                w_copy(i).start()
                i, after = i + 1, after + 1

    late = tiles - EARLY

    def geometry(kind, r):
        if kind == "near":
            return 0, r * BLOCK, BLOCK, 0, tiles, r
        if kind == "early":
            return 1, r * BLOCK, BLOCK, 0, EARLY, blocks + r
        return 1, 0, tokens, r, 1, 2 * blocks + r - EARLY

    def region(kind, r, half=None):
        cb, row, m, c, k, index = geometry(kind, r)
        if half is not None:
            row, m = row + half * (m // 2), m // 2
            row = row if isinstance(row, int) else pl.multiple_of(row, m)
        return cb, pl.ds(row, m), pl.ds(c * tile, k * tile), index

    def product(t, row, m, cb, c, k):
        source = w_far if cb else w

        @pl.loop(c, c + k)
        def _(i):
            cols = pl.ds(pl.multiple_of(i * tile, tile), tile)
            part[t, cb, pl.ds(row, m), cols] = jnp.dot(
                att[t, pl.ds(row, m)], source[:, cols], preferred_element_type=jnp.float32
            ).astype(part.dtype)

    def core_copy(t, kind, r):
        cb, rows, cols, index = region(kind, r)
        return remote(
            part.at[t, cb, rows, cols], rx1.at[t // 2, cb, rows, cols],
            s1.at[t // 2, index], r1.at[t // 2, index], {"sub": away_sub},
        )

    def head_copy(t, kind, r):
        cb, rows, cols, index = region(kind, r, away_head)
        half, short = geometry(kind, r)[1] // 2, geometry(kind, r)[2] // 2
        return remote(
            part.at[t, cb, rows, cols], rx2.at[t // 2, cb, pl.ds(half, short), cols],
            s2.at[t // 2, index], r2.at[t // 2, index], {"head": away_head},
        )

    def is_kept(t, cb):
        if cb:
            return jnp.bool_(False)
        return jnp.logical_and(t == me, keeps)

    def last_copy(t, kind, r):
        cb, rows, cols, index = region(kind, r, head)
        where = {"ctx": t, "head": side, "sub": (me + cb) % 2}
        return remote(
            part.at[t, cb, rows, cols], o_ref.at[rows, cols], s3.at[t // 2, index], r3.at[head, index], where
        )

    def whole_copy(t, kind, r):
        cb, rows, cols, index = region(kind, r)
        where = {"ctx": t, "head": side, "sub": (me + cb) % 2}
        return remote(
            part.at[t, cb, rows, cols], landing.at[head], s3.at[t // 2, index], r3.at[head, index], where
        )

    def is_last(kind, r):
        return kind == "late" and r == tiles - 1

    def keep_copy(t, kind, r):
        cb, rows, cols, index = region(kind, r, head)
        return pltpu.make_async_copy(part.at[t, cb, rows, cols], o_ref.at[rows, cols], s3.at[t // 2, index])

    def owns(t):
        return t % 2 == sub

    def send(jobs):
        for t, kind, r in jobs:
            pl.when(jnp.logical_not(owns(t)))(functools.partial(lambda *a: core_copy(*a).start(), t, kind, r))

    def multiply(*jobs):
        for t, kind, r in jobs:
            cb, row, m, c, k, _ = geometry(kind, r)
            product(t, row, m, cb, c, k)
            send([(t, kind, r)])

    def slab(t, k):
        last = pl.ds((tiles - 1) * tile, tile)
        total = None
        for g in range(2):
            depth = pl.ds(g * (width // 2) + k * (width // 2 // SPLIT), width // 2 // SPLIT)
            term = jnp.dot(att[t, :, depth], w_far[depth, last], preferred_element_type=jnp.float32)
            total = term if total is None else total + term
        return total

    def begin(*toks):
        for t in toks:
            acc[t] = slab(t, 0) + slab(t, 1)

    def extend(*toks):
        for t in toks:
            acc[t] += slab(t, 2)

    def complete(*jobs):
        for t, kind, r in jobs:
            total = acc[t] + slab(t, 3)
            part[t, 1, :, pl.ds((tiles - 1) * tile, tile)] = total.astype(part.dtype)
            send([(t, kind, r)])

    def multiply_all(t, kind):
        cb, _, _, c, k, _ = geometry(kind, 0)
        product(t, 0, tokens, cb, c, k)
        send([(t, kind, r) for r in range(blocks)])

    def combine(*jobs):
        for t, kind, r in jobs:

            @pl.when(owns(t))
            def _():
                cb, rows, cols, _ = region(kind, r)
                core_copy(t, kind, r).wait_recv()
                total = part[t, cb, rows, cols].astype(jnp.float32)
                total += rx1[t // 2, cb, rows, cols].astype(jnp.float32)
                part[t, cb, rows, cols] = total.astype(part.dtype)
                (whole_copy if is_last(kind, r) else head_copy)(t, kind, r).start()

    def finish(*jobs):
        for t, kind, r in jobs:

            @pl.when(owns(t))
            def _():
                cb, rows, cols, _ = region(kind, r, head)
                half, short = geometry(kind, r)[1] // 2, geometry(kind, r)[2] // 2
                head_copy(t, kind, r).wait_recv()
                total = part[t, cb, rows, cols].astype(jnp.float32)
                total += rx2[t // 2, cb, pl.ds(half, short), cols].astype(jnp.float32)
                part[t, cb, rows, cols] = total.astype(part.dtype)
                if cb:
                    last_copy(t, kind, r).start()
                else:
                    pl.when(is_kept(t, cb))(lambda: keep_copy(t, kind, r).start())
                    pl.when(jnp.logical_not(is_kept(t, cb)))(lambda: last_copy(t, kind, r).start())

    def relay_end(r):
        end_copy(r).wait_recv()
        far_copy(end, r).start()

    def await_far(r):
        far_copy(far_end, r).wait_recv()

    def all_rows(t, kind):
        return [(t, kind, r) for r in range(blocks)]

    def both(t, r):
        return [(t, "near", r), (t, "early", r)]

    @pl.when(is_hub)
    def _():
        g0, g1 = all_rows(me, "near"), all_rows(me, "early")
        g2, g5, g9 = both(end, 0), both(end, 1), both(end, 2)
        g3, g4 = all_rows(other, "near"), all_rows(other, "early")
        g6, g7, g11 = both(far_end, 0), both(far_end, 1), both(far_end, 2)

        def late_of(i, *toks):
            return [(t, "late", i) for t in toks]

        g8, g10 = late_of(2, me, other, end), late_of(3, far_end, other, end, me)
        g11 = g11 + late_of(2, far_end)
        g12, g13 = late_of(4, far_end, other), late_of(4, end, me)

        multiply_all(me, "near")
        await_w(*range(8))
        multiply_all(me, "early")
        combine(*g0)
        combine(*g1)
        relay_end(0)
        multiply(*g2)
        combine(*g2)
        finish(*g0)
        finish(*g1)
        for j in range(chunks):
            chunk_copy(other, j).wait_recv()
        multiply_all(other, "near")
        relay_end(1)
        multiply_all(other, "early")
        combine(*g3)
        combine(*g4)
        multiply(*g5)
        finish(*g2)
        combine(*g5)
        await_far(0)
        multiply(*g6)
        relay_end(2)
        combine(*g6)
        multiply(*g9)
        relay_w(8)
        combine(*g9)
        finish(*g3)
        relay_w(9)
        finish(*g4)
        relay_w(10)
        finish(*g5)
        await_far(1)
        multiply(*g7)
        relay_w(11)
        combine(*g7)
        finish(*g6)
        relay_w(12)
        await_w(8, 9, 10, 11)
        relay_w(13)
        multiply(*g8)
        relay_w(14)
        combine(*g8)
        finish(*g9)
        await_far(2)
        multiply(*g11[:2])
        relay_w(15)
        multiply(*g11[2:])
        combine(*g11)
        finish(*g7)
        relay_w(16)
        relay_w(17)
        await_w(12, 13, 14, 15)
        multiply(*g10[:2])
        relay_w(18)
        combine(*g10[:2])
        multiply(*g10[2:3])
        relay_w(19)
        multiply(*g10[3:])
        combine(*g10[2:])
        relay_w(20)
        finish(*g8)
        finish(*g11)
        await_w(16, 17)
        begin(far_end, other, end, me)
        finish(*g10[:2])
        await_w(18)
        extend(far_end, other, end, me)
        await_w(19, 20)
        complete(*g12)
        complete(*g13)
        combine(*g12)
        combine(*g13)
        finish(*g10[2:])

    for way, go in ((0, to_right), (1, to_left)):
        for d in range(n):
            b = me - d if way == 0 else me + d
            fits = b >= 0 if way == 0 else b < n

            @pl.when(jnp.logical_and(fits, go))
            def _():
                for p in range(pairs):
                    kv_copy(b, way, d, p).wait_send()

    @pl.when(is_end)
    def _():
        for i in range(pieces):
            w_copy(i).wait_send()
        for r in range(blocks):
            end_copy(r).wait_send()

    @pl.when(is_hub)
    def _():
        for i in range(pieces):
            y_copy(group, i).wait_send()
        for j in range(chunks):
            chunk_copy(me, j).wait_send()
        for r in range(blocks):
            far_copy(end, r).wait_send()
        names = [("near", r) for r in range(blocks)] + [("early", r) for r in range(blocks)]
        names += [("late", r) for r in range(EARLY, tiles)]
        for t in (me, other, end, far_end):
            for kind, r in names:

                @pl.when(owns(t))
                def _():
                    if is_last(kind, r):
                        whole_copy(t, kind, r).wait_send()
                        return
                    head_copy(t, kind, r).wait_send()
                    if kind == "near":
                        kept = is_kept(t, 0)
                        pl.when(kept)(lambda: keep_copy(t, kind, r).wait())
                        pl.when(jnp.logical_not(kept))(lambda: last_copy(t, kind, r).wait_send())
                    else:
                        last_copy(t, kind, r).wait_send()

                @pl.when(jnp.logical_not(owns(t)))
                def _():
                    core_copy(t, kind, r).wait_send()

    my_cb = (sub + 1 + head) % 2

    def arrivals(cb):
        kinds = [("near", r) for r in range(blocks)]
        if cb:
            kinds = [("early", r) for r in range(blocks)] + [("late", r) for r in range(EARLY, tiles - 1)]
        for kind, r in kinds:
            for h in range(n_head):
                cb_, rows, cols, index = region(kind, r, h)
                got = remote(
                    part.at[0, cb_, rows, cols], o_ref.at[rows, cols], s3.at[0, index], r3.at[h, index],
                    {"ctx": origin, "head": h, "sub": me % 2},
                )
                if cb:
                    got.wait_recv()
                else:
                    pl.when(jnp.logical_not(jnp.logical_and(mine, head == h)))(lambda: got.wait_recv())
        if cb:
            cb_, rows, cols, index = region("late", tiles - 1)
            for h in range(n_head):
                remote(
                    part.at[0, cb_, rows, cols], landing.at[h], s3.at[0, index], r3.at[h, index],
                    {"ctx": origin, "head": h, "sub": me % 2},
                ).wait_recv()
            total = landing[0].astype(jnp.float32)
            for h in range(1, n_head):
                total += landing[h].astype(jnp.float32)
            landing[0] = total.astype(landing.dtype)
            place = pltpu.make_async_copy(landing.at[0], o_ref.at[rows, cols], load_sems.at[0])
            place.start()
            place.wait()

    pl.when(my_cb == 0)(lambda: arrivals(0))
    pl.when(my_cb == 1)(lambda: arrivals(1))


def with_hubs(queries, key_rows, value_rows, out_weight):
    tokens, width = queries.shape
    heads_here = width // HD
    pairs = heads_here // (QH // KVH)
    per_pair = heads_here // pairs
    n = lax.axis_size("ctx")
    n_head = lax.axis_size("head")
    columns = out_weight.shape[1]
    block = (tokens, columns)
    tiles = columns // TILE
    pieces = len(pieces_of(width, tiles))
    blocks = tokens // BLOCK
    kinds = 2 * blocks + tiles - EARLY
    anywhere = pl.BlockSpec(memory_space=pl.ANY)
    dma = pltpu.SemaphoreType.DMA
    bf16 = jnp.bfloat16
    sums = [dma((n // 2, kinds))] * 5 + [dma((n_head, kinds))]
    return pl.pallas_call(
        functools.partial(hub_kernel, n, n_head, per_pair, pairs, CHUNKS, TILE),
        out_shape=jax.ShapeDtypeStruct(block, bf16),
        in_specs=[anywhere] * 4,
        out_specs=anywhere,
        scratch_shapes=[
            pltpu.VMEM((n * tokens, 2 * pairs * HD), bf16),
            pltpu.VMEM((pairs, n * tokens, 2 * HD), bf16),
            pltpu.VMEM((tokens, width), bf16),
            pltpu.VMEM((n, tokens, width), bf16),
            pltpu.VMEM(out_weight.shape, bf16),
            pltpu.VMEM(out_weight.shape, bf16),
            pltpu.VMEM((n, 2) + block, bf16),
            pltpu.VMEM((n // 2, 2) + block, bf16),
            pltpu.VMEM((n // 2, 2, tokens // 2, columns), bf16),
            pltpu.VMEM((n, tokens, TILE), jnp.float32),
            pltpu.VMEM((n_head, tokens, TILE), bf16),
            dma((2 * pairs + 2,)),
            dma((2, n, pairs)),
            dma((n, pairs)),
            dma((CHUNKS,)),
            dma((CHUNKS,)),
            dma((blocks,)),
            dma((blocks,)),
            dma((blocks,)),
            dma((blocks,)),
            dma((pieces,)),
            dma((pieces,)),
            dma((pieces,)),
            dma((pieces,)),
        ] + sums,
        compiler_params=pltpu.CompilerParams(
            collective_id=0, has_side_effects=True, vmem_limit_bytes=60 * 2**20
        ),
    )(key_rows, value_rows, queries, out_weight)


def hubs_fit(mesh, queries, out_weight):
    shape = mesh.shape
    tokens, width = queries[0] // (shape["groups"] * shape["ctx"]), queries[1] // (shape["head"] * shape["sub"])
    columns = out_weight[1] // shape["ctx"]
    sizes = (shape["groups"], shape["ctx"], shape["head"], shape["sub"]) == (2, 4, 2, 2)
    heads = width // HD
    return sizes and tokens == 3 * BLOCK and columns == 5 * TILE and heads == 2 * CHUNKS and heads * KVH == 2 * QH


def solution(mesh):
    assert mesh.shape["sub"] == 2
    assert mesh.shape["ctx"] == mesh.shape["head"] * mesh.shape["sub"]

    def run(queries, key_rows, value_rows, out_weight):
        fits = hubs_fit(mesh, queries.shape, out_weight.shape)
        return jax.shard_map(
            with_hubs if fits else on_device,
            mesh=mesh,
            in_specs=(
                P(("groups", "ctx"), ("head", "sub")),
                P(("groups", "ctx"), "head"),
                P(("groups", "ctx"), "head"),
                P(("head", "sub"), "ctx"),
            ),
            out_specs=P(("groups", "ctx"), ("head", "sub")),
            check_vma=False,
        )(queries, key_rows, value_rows, out_weight)

    return run
```

```python
import functools
import math

import jax
import jax.numpy as jnp
from jax import lax
from jax.experimental import pallas as pl
from jax.experimental.pallas import tpu as pltpu
from jax.sharding import PartitionSpec as P

QH = 64
KVH = 8
HD = 128
CHUNKS = 8
TILE = 256
ROWS = 128
MESH = pl.DeviceIdType.MESH
BLOCK = 128
EARLY = 2
SPLIT = 4
TOGETHER = 4
ORDER = ("w",) * 8 + (0, 1, 2) + ("w",) * 13


def kernel(
    n, n_head, per_pair, pairs, chunks, parts, k_hbm, v_hbm, q_hbm, w_hbm, o_ref,
    kv_all, v_ext, q_ref, att, w, own, out, rx1, summed, rx2, final,
    load_sems, kv_send, kv_recv, a_send, a_recv, s1, r1, s2, r2, s3, r3,
):
    me, head, sub = (lax.axis_index(a) for a in ("ctx", "head", "sub"))
    other = 1 - sub
    hs = head * 2 + sub
    tokens, width = q_ref.shape
    heads = width // HD
    columns = w.shape[1]
    piece = width // chunks
    to_right, to_left = me < n - 1, me > 0
    right, left = lax.min(me + 1, n - 1), lax.max(me - 1, 0)
    away = hs != me
    share = tokens // n_head

    def rows_of(b):
        return pl.ds(pl.multiple_of(b * tokens, tokens), tokens)

    first = pl.multiple_of((sub * heads // (QH // KVH)) * HD, HD)
    loads = [
        pltpu.make_async_copy(
            side.at[:, pl.ds(first, pairs * HD)],
            kv_all.at[rows_of(me), pl.ds(i * pairs * HD, pairs * HD)],
            load_sems.at[i],
        )
        for i, side in enumerate((k_hbm, v_hbm))
    ]
    loads.append(pltpu.make_async_copy(q_hbm, q_ref, load_sems.at[2]))
    loads.append(pltpu.make_async_copy(w_hbm, w, load_sems.at[3]))
    for load in loads:
        load.start()

    barrier = pltpu.get_barrier_semaphore()

    def greet(where):
        pl.semaphore_signal(barrier, inc=1, device_id=where, device_id_type=MESH)

    pl.when(to_right)(lambda: greet({"ctx": right}))
    pl.when(to_left)(lambda: greet({"ctx": left}))
    for h in range(n_head):
        source = {"ctx": hs, "head": h, "sub": me % 2}
        pl.when(jnp.logical_or(away, head != h))(functools.partial(greet, source))
    greet({"sub": other})
    for step in range(1, n_head):
        greet({"head": lax.rem(head + step, n_head)})
    count = 2 * n_head - 1 + to_right.astype(jnp.int32) + to_left.astype(jnp.int32)
    pl.semaphore_wait(barrier, count + away.astype(jnp.int32))

    def remote(src, dst, send, recv, where):
        return pltpu.make_async_remote_copy(
            src_ref=src, dst_ref=dst, send_sem=send, recv_sem=recv, device_id=where, device_id_type=MESH
        )

    def kv_copy(b, way, d):
        where = {"ctx": right if way == 0 else left}
        part = kv_all.at[rows_of(b)]
        return remote(part, part, kv_send.at[way, d], kv_recv.at[b], where)

    loads[0].wait()
    loads[1].wait()
    pl.when(to_right)(lambda: kv_copy(me, 0, 0).start())
    pl.when(to_left)(lambda: kv_copy(me, 1, 0).start())

    @pl.loop(1, n)
    def _(d):
        @pl.when(me - d >= 0)
        def _():
            copy = kv_copy(me - d, 0, d)
            copy.wait_recv()
            pl.when(to_right)(lambda: copy.start())

        @pl.when(me + d < n)
        def _():
            copy = kv_copy(me + d, 1, d)
            copy.wait_recv()
            pl.when(to_left)(lambda: copy.start())

    loads[2].wait()

    def a_copy(b, j, way, d):
        where = {"ctx": right if way == 0 else left}
        part = att.at[b, :, pl.ds(j * piece, piece)]
        return remote(part, part, a_send.at[way, d, j], a_recv.at[b, j], where)

    factor = math.log2(math.e) / HD**0.5
    for j in range(chunks):
        if j % (chunks // pairs) == 0:
            p = j // (chunks // pairs)
            v_ext[p, :, :HD] = kv_all[:, (pairs + p) * HD : (pairs + p + 1) * HD]
            v_ext[p, :, HD:] = jnp.ones((v_ext.shape[1], HD), v_ext.dtype)

        @pl.loop(j * heads // chunks, (j + 1) * heads // chunks)
        def _(h):
            pair = h // per_pair
            cols = pl.ds(pl.multiple_of(h * HD, HD), HD)
            keys = kv_all[:, pl.ds(pl.multiple_of(pair * HD, HD), HD)]
            for start in range(0, tokens, ROWS):
                rows = pl.ds(start, ROWS)
                scores = lax.dot_general(
                    q_ref[rows, cols], keys, (((1,), (1,)), ((), ())), preferred_element_type=jnp.float32
                )
                row_max = jnp.max(scores, axis=1, keepdims=True)
                weights = jnp.exp2((scores - row_max) * factor).astype(jnp.bfloat16)
                both = jnp.dot(weights, v_ext[pair], preferred_element_type=jnp.float32)
                att[me, rows, cols] = (both[:, :HD] / both[:, HD:]).astype(att.dtype)

        pl.when(to_right)(lambda: a_copy(me, j, 0, 0).start())
        pl.when(to_left)(lambda: a_copy(me, j, 1, 0).start())

    loads[3].wait()
    tile = columns // parts

    def cols_of(c):
        return pl.ds(0, columns) if parts == 1 else pl.ds(pl.multiple_of(c * tile, tile), tile)

    def core_copy(g, c):
        cols = cols_of(c)
        return remote(out.at[g, :, cols], rx1.at[g, :, cols], s1.at[g, c], r1.at[g, c], {"sub": other})

    def share_of(h):
        return pl.ds(pl.multiple_of(h * share, share), share)

    def head_copy(g, step, c):
        cols, target = cols_of(c), lax.rem(head + step, n_head)
        return remote(
            summed.at[g, share_of(target), cols], rx2.at[g, head, :, cols],
            s2.at[g, step - 1, c], r2.at[g, head, c], {"head": target},
        )

    def head_arrival(g, source, c):
        cols = cols_of(c)
        return remote(
            summed.at[g, share_of(source), cols], rx2.at[g, source, :, cols],
            s2.at[g, 0, c], r2.at[g, source, c], {"head": source},
        )

    def last_copy(g, h, c):
        cols = cols_of(c)
        where = {"ctx": 2 * g + sub, "head": me // 2, "sub": me % 2}
        return remote(final.at[g, :, cols], o_ref.at[share_of(h), cols], s3.at[g, c], r3.at[h, c], where)

    def product(t, c):
        cols = cols_of(c)
        return jnp.dot(att[t], w[:, cols], preferred_element_type=jnp.float32).astype(out.dtype)

    def multiply(t):
        g = t // 2

        @pl.when(t % 2 == sub)
        def _():
            @pl.loop(0, parts)
            def _(c):
                own[g, :, cols_of(c)] = product(t, c)

        @pl.when(t % 2 != sub)
        def _():
            @pl.loop(0, parts)
            def _(c):
                out[g, :, cols_of(c)] = product(t, c)
                core_copy(g, c).start()

    def combine(t):
        g = t // 2

        @pl.when(t % 2 == sub)
        def _():
            @pl.loop(0, parts)
            def _(c):
                cols = cols_of(c)
                core_copy(g, c).wait_recv()
                total = own[g, :, cols].astype(jnp.float32) + rx1[g, :, cols].astype(jnp.float32)
                summed[g, :, cols] = total.astype(summed.dtype)
                for step in range(1, n_head):
                    head_copy(g, step, c).start()

    def finish(t):
        g = t // 2

        @pl.when(t % 2 == sub)
        def _():
            @pl.loop(0, parts)
            def _(c):
                cols = cols_of(c)
                total = summed[g, share_of(head), cols].astype(jnp.float32)
                for step in range(1, n_head):
                    source = lax.rem(head + step, n_head)
                    head_arrival(g, source, c).wait_recv()
                    total += rx2[g, source, :, cols].astype(jnp.float32)
                final[g, :, cols] = total.astype(final.dtype)
                pl.when(jnp.logical_or(away, t != me))(lambda: last_copy(g, head, c).start())

    def finish_at(d):
        pl.when(jnp.logical_and(d >= 0, me - d >= 0))(lambda: finish(me - d))
        pl.when(jnp.logical_and(d > 0, me + d < n))(lambda: finish(me + d))

    def after(d, j, last=False):
        behind, ahead = me - d + 1, me + d - 1
        if j == 0:
            pl.when(behind >= 0)(lambda: multiply(behind))
        if j == chunks // 4:
            pl.when(jnp.logical_and(ahead < n, d > 1))(lambda: multiply(ahead))
        if j == chunks // 2:
            pl.when(behind >= 0)(lambda: combine(behind))
        if j == chunks // 2 + 1:
            pl.when(jnp.logical_and(ahead < n, d > 1))(lambda: combine(ahead))
        if j == chunks - 1 and not last:
            finish_at(d - 2)

    @pl.loop(1, n)
    def _(d):
        for j in range(chunks):

            @pl.when(me - d >= 0)
            def _():
                copy = a_copy(me - d, j, 0, d)
                copy.wait_recv()
                pl.when(to_right)(lambda: copy.start())

            @pl.when(me + d < n)
            def _():
                copy = a_copy(me + d, j, 1, d)
                copy.wait_recv()
                pl.when(to_left)(lambda: copy.start())

            after(d, j)

    finish_at(n - 2)
    for j in range(chunks):
        after(n, j, last=True)
    finish_at(n - 1)

    @pl.when(jnp.logical_not(away))
    def _():
        keep = pltpu.make_async_copy(final.at[me // 2], o_ref.at[share_of(head)], load_sems.at[0])
        keep.start()
        keep.wait()

    for h in range(n_head):

        @pl.when(jnp.logical_or(away, head != h))
        def _():
            @pl.loop(0, parts)
            def _(c):
                last_copy(0, h, c).wait_recv()

    @pl.loop(0, n)
    def _(d):
        for way, fits, go in ((0, me - d >= 0, to_right), (1, me + d < n, to_left)):
            b = me - d if way == 0 else me + d

            @pl.when(jnp.logical_and(fits, go))
            def _():
                kv_copy(b, way, d).wait_send()
                for j in range(chunks):
                    a_copy(b, j, way, d).wait_send()

    @pl.loop(0, n // 2)
    def _(g):
        @pl.loop(0, parts)
        def _(c):
            core_copy(g, c).wait_send()
            for step in range(1, n_head):
                head_copy(g, step, c).wait_send()
            pl.when(jnp.logical_or(away, 2 * g + sub != me))(lambda: last_copy(g, head, c).wait_send())


def on_device(queries, key_rows, value_rows, out_weight):
    tokens, width = queries.shape
    heads_here = width // HD
    group_ratio = QH // KVH
    pairs = max(heads_here // group_ratio, 1)
    per_pair = heads_here // pairs
    n = lax.axis_size("ctx")
    n_head = lax.axis_size("head")
    columns = out_weight.shape[1]
    block = (tokens, columns)
    groups = (n // 2,) + block
    chunks = min(CHUNKS, heads_here)
    parts = columns // TILE if columns % TILE == 0 else 1
    anywhere = pl.BlockSpec(memory_space=pl.ANY)
    dma = pltpu.SemaphoreType.DMA
    bf16 = jnp.bfloat16
    return pl.pallas_call(
        functools.partial(kernel, n, n_head, per_pair, pairs, chunks, parts),
        out_shape=jax.ShapeDtypeStruct(block, bf16),
        in_specs=[anywhere] * 4,
        out_specs=anywhere,
        scratch_shapes=[
            pltpu.VMEM((n * tokens, 2 * pairs * HD), bf16),
            pltpu.VMEM((pairs, n * tokens, 2 * HD), bf16),
            pltpu.VMEM((tokens, width), bf16),
            pltpu.VMEM((n, tokens, width), bf16),
            pltpu.VMEM(out_weight.shape, bf16),
            pltpu.VMEM(groups, bf16),
            pltpu.VMEM(groups, bf16),
            pltpu.VMEM(groups, bf16),
            pltpu.VMEM(groups, bf16),
            pltpu.VMEM((n // 2, n_head, tokens // n_head, columns), bf16),
            pltpu.VMEM((n // 2, tokens // n_head, columns), bf16),
            dma((4,)),
            dma((2, n)),
            dma((n,)),
            dma((2, n, chunks)),
            dma((n, chunks)),
            dma((n // 2, parts)),
            dma((n // 2, parts)),
            dma((n // 2, n_head - 1, parts)),
            dma((n // 2, n_head, parts)),
            dma((n // 2, parts)),
            dma((n_head, parts)),
        ],
        compiler_params=pltpu.CompilerParams(
            collective_id=0, has_side_effects=True, vmem_limit_bytes=60 * 2**20
        ),
    )(key_rows, value_rows, queries, out_weight)


def pieces_of(width, tiles):
    depth = width // (2 * SPLIT)
    cuts = [(i, k * depth, depth) for i in range(tiles) for k in range(SPLIT)]
    at, row, _ = cuts.pop()
    return cuts + [(at, row, depth // 2), (at, row + depth // 2, depth // 2)]


def hub_kernel(
    n, n_head, per_pair, pairs, chunks, tile, k_hbm, v_hbm, q_hbm, w_hbm, o_ref,
    kv_all, v_ext, q_ref, att, w, w_far, part, rx1, rx2, acc, landing,
    load_sems, kv_send, kv_recv, a_send, a_recv, e_send, e_recv, f_send, f_recv,
    w_send, w_recv, y_send, y_recv, s1, r1, s2, r2, s3, r3,
):
    me, head, sub, group = (lax.axis_index(a) for a in ("ctx", "head", "sub", "groups"))
    tokens, width = q_ref.shape
    heads = width // HD
    columns = w.shape[1]
    blocks = tokens // BLOCK
    tiles = columns // tile
    cuts = pieces_of(width, tiles)
    pieces = len(cuts)
    low = n // 2 - 1
    is_hub = jnp.logical_and(me >= low, me <= low + 1)
    is_end = jnp.logical_not(is_hub)
    to_right, to_left = me < n - 1, me > 0
    right, left = lax.min(me + 1, n - 1), lax.max(me - 1, 0)
    other = n - 1 - me
    end = jnp.where(me <= low, 0, n - 1)
    far_end = n - 1 - end
    my_hub = jnp.where(me <= low, low, low + 1)
    side = me - low
    away_head, away_sub, away_group = 1 - head, 1 - sub, 1 - group

    def rows_of(b):
        return pl.ds(pl.multiple_of(b * tokens, tokens), tokens)

    first = pl.multiple_of((sub * heads // (QH // KVH)) * HD, HD)
    loads = []
    for p in range(pairs):
        for i, ref in enumerate((k_hbm, v_hbm)):
            loads.append(pltpu.make_async_copy(
                ref.at[:, pl.ds(pl.multiple_of(first + p * HD, HD), HD)],
                kv_all.at[rows_of(me), pl.ds((2 * p + i) * HD, HD)],
                load_sems.at[2 * p + i],
            ))
    load_w = pltpu.make_async_copy(w_hbm, w, load_sems.at[2 * pairs])
    load_q = pltpu.make_async_copy(q_hbm, q_ref, load_sems.at[2 * pairs + 1])
    for load in loads + [load_w, load_q]:
        load.start()

    barrier = pltpu.get_barrier_semaphore()

    def greet(where):
        pl.semaphore_signal(barrier, inc=1, device_id=where, device_id_type=MESH)

    pl.when(to_right)(lambda: greet({"ctx": right}))
    pl.when(to_left)(lambda: greet({"ctx": left}))
    greet({"sub": away_sub})
    greet({"head": away_head})
    greet({"groups": away_group})
    origin = low + head
    mine = jnp.logical_and(me == origin, sub == me % 2)
    for h in range(n_head):
        source = {"ctx": origin, "head": h, "sub": me % 2}
        pl.when(jnp.logical_not(jnp.logical_and(mine, head == h)))(functools.partial(greet, source))
    keeps = jnp.logical_and(is_hub, jnp.logical_and(head == side, sub == me % 2))
    count = 3 + to_right.astype(jnp.int32) + to_left.astype(jnp.int32)
    count += jnp.where(is_hub, 4, 0) - keeps.astype(jnp.int32)
    pl.semaphore_wait(barrier, count)

    def remote(src, dst, send, recv, where):
        return pltpu.make_async_remote_copy(
            src_ref=src, dst_ref=dst, send_sem=send, recv_sem=recv, device_id=where, device_id_type=MESH
        )

    def kv_copy(b, way, d, p):
        where = {"ctx": right if way == 0 else left}
        block = kv_all.at[rows_of(b), pl.ds(2 * p * HD, 2 * HD)]
        return remote(block, block, kv_send.at[way, d, p], kv_recv.at[b, p], where)

    for p in range(pairs):
        loads[2 * p].wait()
        loads[2 * p + 1].wait()
        pl.when(to_right)(lambda: kv_copy(me, 0, 0, p).start())
        pl.when(to_left)(lambda: kv_copy(me, 1, 0, p).start())

    def pass_on(d, p):
        @pl.when(me - d >= 0)
        def _():
            copy = kv_copy(me - d, 0, d, p)
            copy.wait_recv()
            pl.when(to_right)(lambda: copy.start())

        @pl.when(me + d < n)
        def _():
            copy = kv_copy(me + d, 1, d, p)
            copy.wait_recv()
            pl.when(to_left)(lambda: copy.start())

    def w_piece(g, i):
        at, row, depth = cuts[i]
        rows = pl.ds(pl.multiple_of(g * (width // 2) + row, depth), depth)
        return rows, pl.ds(at * tile, tile)

    def w_copy(i):
        at = w_piece(group, i)
        return remote(w.at[at], w_far.at[at], w_send.at[i], w_recv.at[i], {"ctx": my_hub})

    def y_copy(g, i):
        at = w_piece(g, i)
        return remote(w_far.at[at], w_far.at[at], y_send.at[i], y_recv.at[i], {"groups": away_group})

    def relay_w(*which):
        for i in which:
            w_copy(i).wait_recv()
            y_copy(group, i).start()

    def await_w(*which):
        for i in which:
            y_copy(away_group, i).wait_recv()

    load_w.wait()
    ahead = ORDER.index(0)

    @pl.when(is_end)
    def _():
        for i in range(ahead):
            w_copy(i).start()

    chunk = width // chunks

    def chunk_copy(b, j):
        at = att.at[b, :, pl.ds(j * chunk, chunk)]
        return remote(at, at, a_send.at[j], a_recv.at[j], {"ctx": other})

    def end_copy(r):
        at = att.at[end, pl.ds(r * BLOCK, BLOCK)]
        return remote(at, at, e_send.at[r], e_recv.at[r], {"ctx": my_hub})

    def far_copy(b, r):
        at = att.at[b, pl.ds(r * BLOCK, BLOCK)]
        return remote(at, at, f_send.at[r], f_recv.at[r], {"ctx": other})

    for d in range(1, n):
        pass_on(d, 0)
        if d == 1:
            for p in range(1, pairs):
                pass_on(d, p)
    load_q.wait()

    factor = math.log2(math.e) / HD**0.5
    per_chunk = heads // chunks

    def prepare(p):
        v_ext[p, :, :HD] = kv_all[:, (2 * p + 1) * HD : (2 * p + 2) * HD]
        v_ext[p, :, HD:] = jnp.ones((v_ext.shape[1], HD), v_ext.dtype)

    def attend(h, p, start):
        rows, cols = pl.ds(start, ROWS), pl.ds(pl.multiple_of(h * HD, HD), HD)
        keys = kv_all[:, 2 * p * HD : (2 * p + 1) * HD]
        scores = lax.dot_general(
            q_ref[rows, cols], keys, (((1,), (1,)), ((), ())), preferred_element_type=jnp.float32
        )
        row_max = jnp.max(scores, axis=1, keepdims=True)
        weights = jnp.exp2((scores - row_max) * factor).astype(jnp.bfloat16)
        both = jnp.dot(weights, v_ext[p], preferred_element_type=jnp.float32)
        att[me, rows, cols] = (both[:, :HD] / both[:, HD:]).astype(att.dtype)

    def rest_of_pairs():
        for d in range(2, n):
            for p in range(1, pairs):
                pass_on(d, p)

    @pl.when(is_hub)
    def _():
        relay_w(0)
        for j in range(chunks):
            p = j * per_chunk // per_pair
            if (j * per_chunk) % per_pair == 0:
                prepare(p)

            @pl.loop(j * per_chunk, (j + 1) * per_chunk)
            def _(h):
                for start in range(0, tokens, ROWS):
                    attend(h, p, start)

            chunk_copy(me, j).start()
            if j == 1:
                rest_of_pairs()
            if j + 1 < chunks:
                relay_w(j + 1)

    @pl.when(is_end)
    def _():
        i = ahead
        prepare(0)
        for r in range(blocks):
            for p in range(pairs):
                if r == 0 and p == 1:
                    rest_of_pairs()
                    for q in range(1, pairs):
                        prepare(q)

                @pl.loop(p * per_pair, (p + 1) * per_pair, step=TOGETHER)
                def _(h):
                    for k in range(TOGETHER):
                        for start in range(r * BLOCK, (r + 1) * BLOCK, ROWS):
                            attend(h + k, p, start)

            end_copy(r).start()
            after = ORDER.index(r) + 1
            while after < len(ORDER) and ORDER[after] == "w":
                w_copy(i).start()
                i, after = i + 1, after + 1

    late = tiles - EARLY

    def geometry(kind, r):
        if kind == "near":
            return 0, r * BLOCK, BLOCK, 0, tiles, r
        if kind == "early":
            return 1, r * BLOCK, BLOCK, 0, EARLY, blocks + r
        return 1, 0, tokens, r, 1, 2 * blocks + r - EARLY

    def region(kind, r, half=None):
        cb, row, m, c, k, index = geometry(kind, r)
        if half is not None:
            row, m = row + half * (m // 2), m // 2
            row = row if isinstance(row, int) else pl.multiple_of(row, m)
        return cb, pl.ds(row, m), pl.ds(c * tile, k * tile), index

    def product(t, row, m, cb, c, k):
        source = w_far if cb else w

        @pl.loop(c, c + k)
        def _(i):
            cols = pl.ds(pl.multiple_of(i * tile, tile), tile)
            part[t, cb, pl.ds(row, m), cols] = jnp.dot(
                att[t, pl.ds(row, m)], source[:, cols], preferred_element_type=jnp.float32
            ).astype(part.dtype)

    def core_copy(t, kind, r):
        cb, rows, cols, index = region(kind, r)
        return remote(
            part.at[t, cb, rows, cols], rx1.at[t // 2, cb, rows, cols],
            s1.at[t // 2, index], r1.at[t // 2, index], {"sub": away_sub},
        )

    def head_copy(t, kind, r):
        cb, rows, cols, index = region(kind, r, away_head)
        half, short = geometry(kind, r)[1] // 2, geometry(kind, r)[2] // 2
        return remote(
            part.at[t, cb, rows, cols], rx2.at[t // 2, cb, pl.ds(half, short), cols],
            s2.at[t // 2, index], r2.at[t // 2, index], {"head": away_head},
        )

    def is_kept(t, cb):
        if cb:
            return jnp.bool_(False)
        return jnp.logical_and(t == me, keeps)

    def last_copy(t, kind, r):
        cb, rows, cols, index = region(kind, r, head)
        where = {"ctx": t, "head": side, "sub": (me + cb) % 2}
        return remote(
            part.at[t, cb, rows, cols], o_ref.at[rows, cols], s3.at[t // 2, index], r3.at[head, index], where
        )

    def whole_copy(t, kind, r):
        cb, rows, cols, index = region(kind, r)
        where = {"ctx": t, "head": side, "sub": (me + cb) % 2}
        return remote(
            part.at[t, cb, rows, cols], landing.at[head], s3.at[t // 2, index], r3.at[head, index], where
        )

    def is_last(kind, r):
        return kind == "late" and r == tiles - 1

    def keep_copy(t, kind, r):
        cb, rows, cols, index = region(kind, r, head)
        return pltpu.make_async_copy(part.at[t, cb, rows, cols], o_ref.at[rows, cols], s3.at[t // 2, index])

    def owns(t):
        return t % 2 == sub

    def send(jobs):
        for t, kind, r in jobs:
            pl.when(jnp.logical_not(owns(t)))(functools.partial(lambda *a: core_copy(*a).start(), t, kind, r))

    def multiply(*jobs):
        for t, kind, r in jobs:
            cb, row, m, c, k, _ = geometry(kind, r)
            product(t, row, m, cb, c, k)
            send([(t, kind, r)])

    def slab(t, k):
        last = pl.ds((tiles - 1) * tile, tile)
        total = None
        for g in range(2):
            depth = pl.ds(g * (width // 2) + k * (width // 2 // SPLIT), width // 2 // SPLIT)
            term = jnp.dot(att[t, :, depth], w_far[depth, last], preferred_element_type=jnp.float32)
            total = term if total is None else total + term
        return total

    def begin(*toks):
        for t in toks:
            acc[t] = slab(t, 0) + slab(t, 1)

    def extend(*toks):
        for t in toks:
            acc[t] += slab(t, 2)

    def complete(*jobs):
        for t, kind, r in jobs:
            total = acc[t] + slab(t, 3)
            part[t, 1, :, pl.ds((tiles - 1) * tile, tile)] = total.astype(part.dtype)
            send([(t, kind, r)])

    def multiply_all(t, kind):
        cb, _, _, c, k, _ = geometry(kind, 0)
        product(t, 0, tokens, cb, c, k)
        send([(t, kind, r) for r in range(blocks)])

    def combine(*jobs):
        for t, kind, r in jobs:

            @pl.when(owns(t))
            def _():
                cb, rows, cols, _ = region(kind, r)
                core_copy(t, kind, r).wait_recv()
                total = part[t, cb, rows, cols].astype(jnp.float32)
                total += rx1[t // 2, cb, rows, cols].astype(jnp.float32)
                part[t, cb, rows, cols] = total.astype(part.dtype)
                (whole_copy if is_last(kind, r) else head_copy)(t, kind, r).start()

    def finish(*jobs):
        for t, kind, r in jobs:

            @pl.when(owns(t))
            def _():
                cb, rows, cols, _ = region(kind, r, head)
                half, short = geometry(kind, r)[1] // 2, geometry(kind, r)[2] // 2
                head_copy(t, kind, r).wait_recv()
                total = part[t, cb, rows, cols].astype(jnp.float32)
                total += rx2[t // 2, cb, pl.ds(half, short), cols].astype(jnp.float32)
                part[t, cb, rows, cols] = total.astype(part.dtype)
                if cb:
                    last_copy(t, kind, r).start()
                else:
                    pl.when(is_kept(t, cb))(lambda: keep_copy(t, kind, r).start())
                    pl.when(jnp.logical_not(is_kept(t, cb)))(lambda: last_copy(t, kind, r).start())

    def relay_end(r):
        end_copy(r).wait_recv()
        far_copy(end, r).start()

    def await_far(r):
        far_copy(far_end, r).wait_recv()

    def all_rows(t, kind):
        return [(t, kind, r) for r in range(blocks)]

    def both(t, r):
        return [(t, "near", r), (t, "early", r)]

    @pl.when(is_hub)
    def _():
        g0, g1 = all_rows(me, "near"), all_rows(me, "early")
        g2, g5, g9 = both(end, 0), both(end, 1), both(end, 2)
        g3, g4 = all_rows(other, "near"), all_rows(other, "early")
        g6, g7, g11 = both(far_end, 0), both(far_end, 1), both(far_end, 2)

        def late_of(i, *toks):
            return [(t, "late", i) for t in toks]

        g8, g10 = late_of(2, me, other, end), late_of(3, far_end, other, end, me)
        g11 = g11 + late_of(2, far_end)
        g12, g13 = late_of(4, far_end, other), late_of(4, end, me)

        multiply_all(me, "near")
        await_w(*range(8))
        multiply_all(me, "early")
        combine(*g0)
        combine(*g1)
        relay_end(0)
        multiply(*g2)
        combine(*g2)
        finish(*g0)
        finish(*g1)
        for j in range(chunks):
            chunk_copy(other, j).wait_recv()
        multiply_all(other, "near")
        relay_end(1)
        multiply_all(other, "early")
        combine(*g3)
        combine(*g4)
        multiply(*g5)
        finish(*g2)
        combine(*g5)
        await_far(0)
        multiply(*g6)
        relay_end(2)
        combine(*g6)
        multiply(*g9)
        relay_w(8)
        combine(*g9)
        finish(*g3)
        relay_w(9)
        finish(*g4)
        relay_w(10)
        finish(*g5)
        await_far(1)
        multiply(*g7)
        relay_w(11)
        combine(*g7)
        finish(*g6)
        relay_w(12)
        await_w(8, 9, 10, 11)
        relay_w(13)
        multiply(*g8)
        relay_w(14)
        combine(*g8)
        finish(*g9)
        await_far(2)
        multiply(*g11[:2])
        relay_w(15)
        multiply(*g11[2:])
        combine(*g11)
        finish(*g7)
        relay_w(16)
        relay_w(17)
        await_w(12, 13, 14, 15)
        multiply(*g10[:2])
        relay_w(18)
        multiply(*g10[2:])
        relay_w(19)
        combine(*g10)
        relay_w(20)
        finish(*g8)
        finish(*g11)
        await_w(16, 17)
        begin(far_end, other, end, me)
        await_w(18)
        extend(far_end, other, end, me)
        finish(*g10)
        await_w(19, 20)
        complete(*g12)
        complete(*g13)
        combine(*g12)
        combine(*g13)

    for way, go in ((0, to_right), (1, to_left)):
        for d in range(n):
            b = me - d if way == 0 else me + d
            fits = b >= 0 if way == 0 else b < n

            @pl.when(jnp.logical_and(fits, go))
            def _():
                for p in range(pairs):
                    kv_copy(b, way, d, p).wait_send()

    @pl.when(is_end)
    def _():
        for i in range(pieces):
            w_copy(i).wait_send()
        for r in range(blocks):
            end_copy(r).wait_send()

    @pl.when(is_hub)
    def _():
        for i in range(pieces):
            y_copy(group, i).wait_send()
        for j in range(chunks):
            chunk_copy(me, j).wait_send()
        for r in range(blocks):
            far_copy(end, r).wait_send()
        names = [("near", r) for r in range(blocks)] + [("early", r) for r in range(blocks)]
        names += [("late", r) for r in range(EARLY, tiles)]
        for t in (me, other, end, far_end):
            for kind, r in names:

                @pl.when(owns(t))
                def _():
                    if is_last(kind, r):
                        whole_copy(t, kind, r).wait_send()
                        return
                    head_copy(t, kind, r).wait_send()
                    if kind == "near":
                        kept = is_kept(t, 0)
                        pl.when(kept)(lambda: keep_copy(t, kind, r).wait())
                        pl.when(jnp.logical_not(kept))(lambda: last_copy(t, kind, r).wait_send())
                    else:
                        last_copy(t, kind, r).wait_send()

                @pl.when(jnp.logical_not(owns(t)))
                def _():
                    core_copy(t, kind, r).wait_send()

    my_cb = (sub + 1 + head) % 2

    def arrivals(cb):
        kinds = [("near", r) for r in range(blocks)]
        if cb:
            kinds = [("early", r) for r in range(blocks)] + [("late", r) for r in range(EARLY, tiles - 1)]
        for kind, r in kinds:
            for h in range(n_head):
                cb_, rows, cols, index = region(kind, r, h)
                got = remote(
                    part.at[0, cb_, rows, cols], o_ref.at[rows, cols], s3.at[0, index], r3.at[h, index],
                    {"ctx": origin, "head": h, "sub": me % 2},
                )
                if cb:
                    got.wait_recv()
                else:
                    pl.when(jnp.logical_not(jnp.logical_and(mine, head == h)))(lambda: got.wait_recv())
        if cb:
            cb_, rows, cols, index = region("late", tiles - 1)
            for h in range(n_head):
                remote(
                    part.at[0, cb_, rows, cols], landing.at[h], s3.at[0, index], r3.at[h, index],
                    {"ctx": origin, "head": h, "sub": me % 2},
                ).wait_recv()
            total = landing[0].astype(jnp.float32)
            for h in range(1, n_head):
                total += landing[h].astype(jnp.float32)
            landing[0] = total.astype(landing.dtype)
            place = pltpu.make_async_copy(landing.at[0], o_ref.at[rows, cols], load_sems.at[0])
            place.start()
            place.wait()

    pl.when(my_cb == 0)(lambda: arrivals(0))
    pl.when(my_cb == 1)(lambda: arrivals(1))


def with_hubs(queries, key_rows, value_rows, out_weight):
    tokens, width = queries.shape
    heads_here = width // HD
    pairs = heads_here // (QH // KVH)
    per_pair = heads_here // pairs
    n = lax.axis_size("ctx")
    n_head = lax.axis_size("head")
    columns = out_weight.shape[1]
    block = (tokens, columns)
    tiles = columns // TILE
    pieces = len(pieces_of(width, tiles))
    blocks = tokens // BLOCK
    kinds = 2 * blocks + tiles - EARLY
    anywhere = pl.BlockSpec(memory_space=pl.ANY)
    dma = pltpu.SemaphoreType.DMA
    bf16 = jnp.bfloat16
    sums = [dma((n // 2, kinds))] * 5 + [dma((n_head, kinds))]
    return pl.pallas_call(
        functools.partial(hub_kernel, n, n_head, per_pair, pairs, CHUNKS, TILE),
        out_shape=jax.ShapeDtypeStruct(block, bf16),
        in_specs=[anywhere] * 4,
        out_specs=anywhere,
        scratch_shapes=[
            pltpu.VMEM((n * tokens, 2 * pairs * HD), bf16),
            pltpu.VMEM((pairs, n * tokens, 2 * HD), bf16),
            pltpu.VMEM((tokens, width), bf16),
            pltpu.VMEM((n, tokens, width), bf16),
            pltpu.VMEM(out_weight.shape, bf16),
            pltpu.VMEM(out_weight.shape, bf16),
            pltpu.VMEM((n, 2) + block, bf16),
            pltpu.VMEM((n // 2, 2) + block, bf16),
            pltpu.VMEM((n // 2, 2, tokens // 2, columns), bf16),
            pltpu.VMEM((n, tokens, TILE), jnp.float32),
            pltpu.VMEM((n_head, tokens, TILE), bf16),
            dma((2 * pairs + 2,)),
            dma((2, n, pairs)),
            dma((n, pairs)),
            dma((CHUNKS,)),
            dma((CHUNKS,)),
            dma((blocks,)),
            dma((blocks,)),
            dma((blocks,)),
            dma((blocks,)),
            dma((pieces,)),
            dma((pieces,)),
            dma((pieces,)),
            dma((pieces,)),
        ] + sums,
        compiler_params=pltpu.CompilerParams(
            collective_id=0, has_side_effects=True, vmem_limit_bytes=60 * 2**20
        ),
    )(key_rows, value_rows, queries, out_weight)


def hubs_fit(mesh, queries, out_weight):
    shape = mesh.shape
    tokens, width = queries[0] // (shape["groups"] * shape["ctx"]), queries[1] // (shape["head"] * shape["sub"])
    columns = out_weight[1] // shape["ctx"]
    sizes = (shape["groups"], shape["ctx"], shape["head"], shape["sub"]) == (2, 4, 2, 2)
    heads = width // HD
    return sizes and tokens == 3 * BLOCK and columns == 5 * TILE and heads == 2 * CHUNKS and heads * KVH == 2 * QH


def solution(mesh):
    assert mesh.shape["sub"] == 2
    assert mesh.shape["ctx"] == mesh.shape["head"] * mesh.shape["sub"]

    def run(queries, key_rows, value_rows, out_weight):
        fits = hubs_fit(mesh, queries.shape, out_weight.shape)
        return jax.shard_map(
            with_hubs if fits else on_device,
            mesh=mesh,
            in_specs=(
                P(("groups", "ctx"), ("head", "sub")),
                P(("groups", "ctx"), "head"),
                P(("groups", "ctx"), "head"),
                P(("head", "sub"), "ctx"),
            ),
            out_specs=P(("groups", "ctx"), ("head", "sub")),
            check_vma=False,
        )(queries, key_rows, value_rows, out_weight)

    return run
```
